256 devices in a mesh: role: 2 (over x_hi), seq: 16 (over z, core), head: 8 (over x_lo, y).
Axes of the slice: x: 4 (x_hi: 2, x_lo: 2; x = x_hi * 2 + x_lo), y: 4, z: 8, core: 2. Of those that a mesh axis runs over, the one named last changes fastest.
Arguments:
- hidden_rows: bfloat16 [6144, 5120], P('seq'), may hold values from -6 to 6
- gen_weight: bfloat16 [5120, 5120], P(None, ('role', 'head')), may hold values from -0.078125 to 0.078125
- noise: bfloat16 [6144, 5120], P('seq'), may hold values from -6 to 6
- timesteps: int32 [96], P('seq'), may hold values from 20 to 979
- qkv_weight: bfloat16 [2, 5120, 9216], P('role', 'seq', 'head'), may hold values from -0.078125 to 0.078125
- out_weight: bfloat16 [2, 3072, 5120], P('role', 'head'), may hold values from -0.109375 to 0.109375
- qk_gain: float32 [2, 2, 24], P('role', None, 'head'), may hold values from 0.6 to 9
- block_keys: int32 [24, 96, 8], P('head', 'seq'), may hold values from 0 to 95, as said below
- block_count: int32 [24, 96], P('head', 'seq'), may hold values from 1 to 8, as said below
Outputs:
- score_grad: float32 [6144, 5120], P('seq', ('role', 'head'))
The draws below stay inside these ranges and needn't reach their ends.
Inputs may be any that keep to these rules, and one draw needn't show every extreme that they name: `block_keys`: entry 0 of each list is the query block itself; the entries of one list are distinct. For each head, all entries of the lists of one index of seq name at most 2 distinct blocks of any other index of seq, and every index names exactly 2 blocks of the next index. `block_count`: in every draw the lists of some sequence shards are all full, those of others shorter.
All inputs are finite; a program needn't handle non-finite values.
Results may differ from the reference program's by a relative error of at most 0.018.
The reference program's roundings to bfloat16 on the way count: a program that leaves them out, or rounds other values in their place, can miss the bound.
Values may be sent and summed in bfloat16 or wider, within the bound.
A program may use at most 128 MiB of HBM per device.

```python
import math
import jax
import jax.numpy as jnp
from jax import lax

D = 5120
HEADS = 24
HEAD_DIM = 128
BLOCK = 64
KMAX = 8
TOK_DEV = 384
TOKENS = 6144
BLOCKS = 96
CAP = 2


def draw_qk_gain(key, part):
    upper = math.log(2.2)
    return jnp.exp(jax.random.uniform(key, (2, 2, HEADS), jnp.float32, math.log(0.6), upper))


def pair_lists(key):
    blocks = TOKENS // BLOCK
    shard_blocks = TOK_DEV // BLOCK
    shards = TOKENS // TOK_DEV
    width = shard_blocks + shards * CAP
    elig_scores = jax.random.randint(jax.random.fold_in(key, 17), (HEADS, shards, shards, shard_blocks), 0, 1 << 20)
    elig_rank = elig_scores * shard_blocks + lax.broadcasted_iota(jnp.int32, (HEADS, shards, shards, shard_blocks), 3)
    owner_grid = lax.broadcasted_iota(jnp.int32, (HEADS, shards, shards, CAP), 2)
    eligible = lax.top_k(elig_rank, CAP)[1].astype(jnp.int32) + owner_grid * shard_blocks
    own_blocks = lax.broadcasted_iota(jnp.int32, (HEADS, shards, shard_blocks), 1) * shard_blocks + lax.broadcasted_iota(jnp.int32, (HEADS, shards, shard_blocks), 2)
    candidates = jnp.concatenate([own_blocks, eligible.reshape(HEADS, shards, shards * CAP)], axis=2)
    dest_grid = lax.broadcasted_iota(jnp.int32, (HEADS, shards, shards, CAP), 1)
    remote_ok = (owner_grid != dest_grid).reshape(HEADS, shards, shards * CAP)
    next_one = (owner_grid == (dest_grid + 1) % shards).reshape(HEADS, shards, shards * CAP)
    valid = jnp.concatenate([jnp.ones((HEADS, shards, shard_blocks), bool), remote_ok], axis=2)
    forced = jnp.concatenate([jnp.zeros((HEADS, shards, shard_blocks), bool), next_one], axis=2)
    cand_b = jnp.repeat(candidates, shard_blocks, axis=1)
    valid_b = jnp.repeat(valid, shard_blocks, axis=1)
    forced_b = jnp.repeat(forced, shard_blocks, axis=1)
    anchor_b = lax.broadcasted_iota(jnp.int32, (HEADS, blocks, width), 1)
    valid_b = jnp.logical_and(valid_b, cand_b != anchor_b)
    first_b = anchor_b % shard_blocks == 0
    forced_b = jnp.logical_and(forced_b, first_b)
    pick_scores = jax.random.randint(jax.random.fold_in(key, 23), (HEADS, blocks, width), 0, 1 << 20)
    pick_scores = pick_scores * width + lax.broadcasted_iota(jnp.int32, (HEADS, blocks, width), 2)
    pick_scores = jnp.where(forced_b, pick_scores + (1 << 28), pick_scores)
    pick_scores = jnp.where(valid_b, pick_scores, -1)
    picked = lax.top_k(pick_scores, KMAX - 1)[1].astype(jnp.int32)
    chosen = jnp.take_along_axis(cand_b, picked, axis=2)
    anchor = lax.broadcasted_iota(jnp.int32, (HEADS, blocks, 1), 1)
    key_list = jnp.concatenate([anchor, chosen], axis=2).astype(jnp.int32)
    heavy = jax.random.randint(jax.random.fold_in(key, 29), (shards,), 0, 3) == 0
    heavy = jnp.logical_or(heavy, lax.broadcasted_iota(jnp.int32, (shards,), 0) == 0)
    shard_of = lax.broadcasted_iota(jnp.int32, (blocks,), 0) // shard_blocks
    heavy_blocks = jnp.any(jnp.logical_and(shard_of[:, None] == lax.broadcasted_iota(jnp.int32, (blocks, shards), 1), heavy[None, :]), axis=1)
    light = jax.random.randint(jax.random.fold_in(key, 31), (HEADS, blocks), 1, KMAX // 2 + 1)
    counts = jnp.where(heavy_blocks[None, :], KMAX, light).astype(jnp.int32)
    return (key_list, counts)


def draw_block_keys(key, part):
    return pair_lists(key)[0]


def draw_block_count(key, part):
    return pair_lists(key)[1]


def touch_ends(entries, stream_key, least, largest):
    shape = entries.shape
    spot = [jax.random.randint(jax.random.fold_in(stream_key, axis), (), 0, shape[axis]) for axis in range(len(shape))]
    entries = entries.at[tuple(spot)].set(least)
    longest = shape.index(max(shape))
    spot[longest] = (spot[longest] + 1) % shape[longest]
    return entries.at[tuple(spot)].set(largest)


def steps_of(key, dims, cuts, least, high):
    gain, own = 1.0, jax.random.fold_in(key, 6)
    for dim, blocks in cuts:
        steps = jnp.exp(jax.random.uniform(jax.random.fold_in(own, dim), (blocks,), jnp.float32, least / len(cuts), high / len(cuts)))
        gain = gain * jnp.repeat(steps, dims[dim] // blocks).reshape([-1 if axis == dim else 1 for axis in range(len(dims))])
    return gain


def gaussian(stream_key, dims, scale, limit, cuts=(), held_as=jnp.bfloat16):
    result = jax.random.normal(stream_key, dims, jnp.float32) * scale
    if len(cuts) > 0:
        result = steps_of(stream_key, dims, cuts, -0.22, 0.18) * result
    return jnp.clip(result, min=-limit, max=limit).astype(held_as)


def setup_inputs(seed: int = 0) -> dict:
    streams_of = jax.random.split(jax.random.key(seed), 10)
    return {
        "hidden_rows": gaussian(streams_of[0], (TOKENS, D), 1.0, 6.0, ((0, 16),)),
        "gen_weight": gaussian(streams_of[1], (D, D), D ** -0.5, 0.078125, ((1, 16),)),
        "noise": gaussian(streams_of[2], (TOKENS, D), 1.0, 6.0, ((0, 16),)),
        "timesteps": touch_ends(jax.random.randint(streams_of[3], (BLOCKS,), 20, 980), jax.random.fold_in(streams_of[3], 1), 20, 979).astype(jnp.int32),
        "qkv_weight": gaussian(streams_of[4], (2, D, 3 * HEADS * HEAD_DIM), D ** -0.5, 0.078125, ((0, 2), (1, 16), (2, 8))),
        "out_weight": gaussian(streams_of[5], (2, HEADS * HEAD_DIM, D), (HEADS * HEAD_DIM) ** -0.5, 0.109375, ((0, 2), (1, 8))),
        "qk_gain": draw_qk_gain(jax.random.fold_in(streams_of[9], 71), 0),
        "block_keys": draw_block_keys(jax.random.fold_in(streams_of[9], 71), 0),
        "block_count": draw_block_count(jax.random.fold_in(streams_of[9], 71), 0),
    }


def rms_rows(values):
    return values * lax.rsqrt(lax.optimization_barrier(jnp.mean(values * values, axis=-1, keepdims=True)) + 1e-06)

def block_attention(operands):
    queries, key_table, value_table, key_list, key_count = operands
    picked_keys = key_table[key_list]
    picked_values = value_table[key_list]
    scale = 1.0 / math.sqrt(HEAD_DIM)
    scores = jnp.einsum('nqe,nkbe->nqkb', queries.astype(jnp.float32), picked_keys.astype(jnp.float32)) * scale
    live = jnp.arange(KMAX)[None, :] < key_count[:, None]
    scores = jnp.where(live[:, None, :, None], scores, -jnp.inf)
    highest = lax.optimization_barrier(jnp.max(scores, axis=(2, 3), keepdims=True))
    raised = jnp.exp(scores - highest)
    summed = lax.optimization_barrier(jnp.sum(raised, axis=(2, 3), keepdims=True))
    weights = (raised / summed).astype(jnp.bfloat16)
    mixed = jnp.einsum('nqkb,nkbe->nqe', weights.astype(jnp.float32), picked_values.astype(jnp.float32))
    return mixed.astype(jnp.bfloat16)

def section_output(normed, weight_one, out_one, gain_one, block_keys, block_count):
    projected = jnp.dot(normed, weight_one, preferred_element_type=jnp.float32)
    projected = projected.reshape(TOKENS, HEADS, 3, HEAD_DIM)
    queries = (rms_rows(projected[:, :, 0]) * gain_one[0][None, :, None]).astype(jnp.bfloat16)
    key_rows = (rms_rows(projected[:, :, 1]) * gain_one[1][None, :, None]).astype(jnp.bfloat16)
    value_rows = projected[:, :, 2].astype(jnp.bfloat16)

    def by_head(array):
        return array.reshape(BLOCKS, BLOCK, HEADS, HEAD_DIM).transpose(2, 0, 1, 3)
    attended = lax.map(block_attention, (by_head(queries), by_head(key_rows), by_head(value_rows), block_keys, block_count))
    attended = attended.transpose(1, 2, 0, 3).reshape(TOKENS, HEADS * HEAD_DIM)
    return jnp.dot(attended, out_one, preferred_element_type=jnp.float32)

def reference(hidden_rows, gen_weight, noise, timesteps, qkv_weight, out_weight, qk_gain, block_keys, block_count):
    generated = jnp.dot(hidden_rows, gen_weight, preferred_element_type=jnp.float32).astype(jnp.bfloat16)
    angle_rows = jnp.repeat(timesteps.astype(jnp.float32) * (math.pi / 2000.0), BLOCK)[:, None]
    noisy = jnp.cos(angle_rows) * generated.astype(jnp.float32) + jnp.sin(angle_rows) * noise.astype(jnp.float32)
    normed = rms_rows(noisy).astype(jnp.bfloat16)
    real_term = section_output(normed, qkv_weight[0], out_weight[0], qk_gain[0], block_keys, block_count)
    fake_term = section_output(normed, qkv_weight[1], out_weight[1], qk_gain[1], block_keys, block_count)
    return fake_term - real_term
```

```python
import math

import jax
import jax.numpy as jnp
from jax import lax
from jax.experimental import pallas as pl
from jax.experimental.pallas import tpu as pltpu
from jax.sharding import PartitionSpec as P

HEAD_DIM = 128
BLOCK = 64
KMAX = 8
ROWS = 384
D = 5120
SLICE = 320
NX, NY, NZ = 4, 4, 8
HEADS_HERE = 3
MESH = pl.DeviceIdType.MESH
F32 = jnp.float32
BF16 = jnp.bfloat16


def rms(values):
    return values * lax.rsqrt(jnp.mean(values * values, axis=-1, keepdims=True) + 1e-06)


def kernel(
    angles, gain, keys, count,
    hidden, gen_w, noise, qkv_w, out_w,
    out,
    hid, gw, nz, xg, wb, qt, kv0, kv1, kv2, sl, wo, at, acc, oacc,
    loc_sem, zs, zr, ps, pr, xs, xr, ws, wr,
):
    kv = (kv0, kv1, kv2)
    role = lax.axis_index("role")
    seq = lax.axis_index("seq")
    head = lax.axis_index("head")
    z, c = seq // 2, seq % 2
    x = role * 2 + head // 4
    y = head % 4
    me = x * NY + y

    def at_x(d):
        xx = (x + d + NX) % NX
        return {"role": xx // 2, "head": (xx % 2) * 4 + y}

    def at_y(d):
        return {"head": (head // 4) * 4 + (y + d + NY) % NY}

    def at_z(d):
        return {"seq": ((z + d + NZ) % NZ) * 2 + c}

    def plane(i):
        j = (me + i) % 16
        return {"role": j // 8, "head": j % 8}

    partner = {"seq": z * 2 + 1 - c}

    def local(src, dst, i):
        cp = pltpu.make_async_copy(src, dst, loc_sem.at[i])
        cp.start()
        return cp

    w_own = [
        local(qkv_w.at[0, :, pl.ds(h * ROWS, ROWS)], wb.at[h, z, c], h)
        for h in range(HEADS_HERE)
    ]
    hid_cp = local(hidden, hid, 3)
    gw_cp = local(gen_w, gw, 4)
    nz_cp = local(noise, nz, 5)

    barrier = pltpu.get_barrier_semaphore()
    for d in (1, -1):
        pl.semaphore_signal(barrier, inc=1, device_id=at_z(d), device_id_type=MESH)
    pl.semaphore_signal(barrier, inc=1, device_id=partner, device_id_type=MESH)

    def greet(i, carry):
        pl.semaphore_signal(barrier, inc=1, device_id=plane(i), device_id_type=MESH)
        return carry

    lax.fori_loop(1, 16, greet, 0)
    pl.semaphore_wait(barrier, 18)

    started = []

    def send(src, dst, ssem, rsem, device):
        cp = pltpu.make_async_remote_copy(
            src_ref=src, dst_ref=dst, send_sem=ssem, recv_sem=rsem,
            device_id=device, device_id_type=MESH,
        )
        cp.start()
        started.append(cp)
        return cp

    class Ring:
        def __init__(self, g, part, whole):
            self.g, self.part, self.whole = g, part, whole
            self.cp = {}

        def push(self, way, half, k):
            shard = (z + NZ - way * (k - 1)) % NZ
            i = (0 if way > 0 else 7) + (k - 1 if half == 0 else (4 if way > 0 else 3) + k - 1)
            ref = self.part(shard, half)
            self.cp[way, half, k] = send(
                ref, ref, zs.at[self.g, i], zr.at[self.g, i], at_z(way)
            )

        def give(self, d):
            ref = self.whole((z + d + NZ) % NZ)
            n = d + 3
            self.cp["p", d] = send(ref, ref, ps.at[self.g, n], pr.at[self.g, n], partner)

        def own(self):
            self.push(1, 0, 1)
            self.push(-1, 1, 1)
            self.push(1, 1, 1)
            self.push(-1, 0, 1)
            self.give(0)

        def step(self, k):
            if k < 4:
                for way, half in ((1, 0), (-1, 1)):
                    self.cp[way, half, k].wait_recv()
                    self.push(way, half, k + 1)
                for way, half in ((1, 1), (-1, 0)):
                    self.cp[way, half, k].wait_recv()
                    if k < 3:
                        self.push(way, half, k + 1)
                self.give(-k)
                self.give(k)
            else:
                self.cp[1, 0, 4].wait_recv()
                self.cp[-1, 1, 4].wait_recv()
                self.give(4)

        def finish(self):
            for d in range(-3, 5):
                self.cp["p", d].wait_recv()

    def w_ring(h):
        return Ring(
            h,
            lambda zz, half: wb.at[h, zz, c, pl.ds(half * 160, 160)],
            lambda zz: wb.at[h, zz, c],
        )

    def kv_ring(h):
        return Ring(
            3 + h,
            lambda zz, half: kv[h].at[zz, c, pl.ds(half * 3, 3)],
            lambda zz: kv[h].at[zz, c],
        )

    class Plane:
        def __init__(self, g, buf):
            self.g, self.buf = g, buf
            self.n = 0
            self.cp = {}

        def push(self, name, ref, device):
            self.cp[name] = send(
                ref, ref, xs.at[self.g, self.n], xr.at[self.g, self.n], device
            )
            self.n += 1

        def start(self):
            b = self.buf
            for d in (1, -1):
                self.push(("a1", d), b.at[x, y, pl.ds(0, 192)], at_x(d))
                self.push(("b1", d), b.at[x, y, pl.ds(192, 192)], at_y(d))

        def one(self):
            b = self.buf
            for n, d in enumerate((1, -1)):
                self.cp["a1", d].wait_recv()
                self.push(("a2", d), b.at[(x - d + NX) % NX, y, pl.ds(n * 96, 96)], at_x(d))
                self.cp["b1", d].wait_recv()
                self.push(("b2", d), b.at[x, (y - d + NY) % NY, pl.ds(192 + n * 96, 96)], at_y(d))

        def two(self):
            b = self.buf
            for d in (1, -1):
                self.cp["a2", d].wait_recv()
            for d in (1, -1):
                self.push(("a3", d), b.at[:, y, pl.ds(0, 192)], at_y(d))
            for d in (1, -1):
                self.cp["b2", d].wait_recv()
            for d in (1, -1):
                self.push(("b3", d), b.at[x, :, pl.ds(192, 192)], at_x(d))

        def three(self):
            b = self.buf
            for n, d in enumerate((1, -1)):
                self.cp["a3", d].wait_recv()
                self.push(
                    ("a4", d), b.at[pl.ds(2 * n, 2), (y - d + NY) % NY, pl.ds(0, 192)], at_y(d)
                )
                self.cp["b3", d].wait_recv()
                self.push(
                    ("b4", d), b.at[(x - d + NX) % NX, pl.ds(2 * n, 2), pl.ds(192, 192)], at_x(d)
                )

        def four(self):
            for d in (1, -1):
                self.cp["a4", d].wait_recv()
                self.cp["b4", d].wait_recv()

    wr_ = [w_ring(h) for h in range(HEADS_HERE)]
    kr_ = [kv_ring(h) for h in range(HEADS_HERE)]
    gx = Plane(0, xg)
    ax = [Plane(1 + h, at.at[h]) for h in range(HEADS_HERE)]

    for h in range(HEADS_HERE):
        w_own[h].wait()
        if h < 2:
            wr_[h].own()

    hid_cp.wait()
    gw_cp.wait()
    acc[:, :SLICE] = jnp.zeros((ROWS, SLICE), F32)

    def gen_step(i, carry):
        k0 = pl.multiple_of(i * 1024, 1024)
        acc[:, :SLICE] += jnp.dot(
            hid[:, pl.ds(k0, 1024)], gw[pl.ds(k0, 1024), :], preferred_element_type=F32
        )
        return carry

    lax.fori_loop(0, D // 1024, gen_step, 0)
    xg[x, y] = acc[:, :SLICE].astype(BF16)
    gx.start()
    wr_[0].step(1)
    ow_cp = local(out_w.at[0], hid, 6)
    gx.one()
    wr_[1].step(1)
    gx.two()

    ow_cp.wait()
    for j in range(16):
        sl[j] = hid[:, j * SLICE:(j + 1) * SLICE].reshape(HEADS_HERE, 128, SLICE)

    wr_[0].step(2)
    wr_[2].own()
    wr_[1].step(2)
    gx.three()
    gx.four()

    half = pl.ds(c * 64, 64)
    wo_own = pltpu.make_async_copy(sl.at[me, :, half], wo.at[:, me, half], loc_sem.at[7])
    wo_own.start()

    def wo_copy(i):
        j = (me + i) % 16
        return pltpu.make_async_remote_copy(
            src_ref=sl.at[j, :, half], dst_ref=wo.at[:, me, half],
            send_sem=ws.at[i], recv_sem=wr.at[i],
            device_id=plane(i), device_id_type=MESH,
        )

    def wo_start(i, carry):
        wo_copy(i).start()
        return carry

    lax.fori_loop(1, 16, wo_start, 0)

    nz_cp.wait()
    for cp in gx.cp.values():
        cp.wait_send()
    drained = {id(cp) for cp in gx.cp.values()}

    def norm_step(b, carry):
        rows = pl.ds(pl.multiple_of(b * BLOCK, BLOCK), BLOCK)
        ca, sa = angles[0, b], angles[1, b]

        def noisy(j):
            g = xg[j // NY, j % NY, rows, :].astype(F32)
            n = nz[rows, j * SLICE:(j + 1) * SLICE].astype(F32)
            return ca * g + sa * n

        total = jnp.zeros((BLOCK, 1), F32)
        for j in range(16):
            v = noisy(j)
            total = total + jnp.sum(v * v, axis=-1, keepdims=True)
        inv = lax.rsqrt(total * (1.0 / D) + 1e-06)
        for j in range(16):
            xg[j // NY, j % NY, rows, :] = (noisy(j) * inv).astype(BF16)
        return carry

    lax.fori_loop(0, ROWS // BLOCK, norm_step, 0)

    def project(h):
        acc[...] = jnp.zeros((ROWS, ROWS), F32)

        def proj_step(zz, carry):
            part = jnp.zeros((ROWS, ROWS), F32)
            for cc in range(2):
                s = zz * 2 + cc
                part = part + jnp.dot(
                    xg[s // NY, s % NY], wb[h, zz, cc], preferred_element_type=F32
                )
            acc[...] += part
            return carry

        lax.fori_loop(0, NZ, proj_step, 0)
        q = (rms(acc[:, 0:128]) * gain[0, 0, h]).astype(BF16)
        k = (rms(acc[:, 128:256]) * gain[0, 1, h]).astype(BF16)
        v = acc[:, 256:384].astype(BF16)
        qt[h] = q.reshape(6, BLOCK, HEAD_DIM)
        kv[h][z, c, :, :, 0:128] = k.reshape(6, BLOCK, HEAD_DIM)
        kv[h][z, c, :, :, 128:256] = v.reshape(6, BLOCK, HEAD_DIM)

    sign = (2 * role - 1).astype(F32)
    scale = 1.0 / math.sqrt(HEAD_DIM)

    def attend(h):
        def two_blocks(b2, carry):
            for u in range(2):
                b = b2 * 2 + u
                q = qt[h, b]
                got = []
                for j in range(KMAX):
                    kb = keys[h, b, j]
                    s = kb // 6
                    got.append(kv[h][s // 2, s % 2, kb - s * 6])
                both = jnp.concatenate(got, axis=0)
                s = lax.dot_general(
                    q, both[:, 0:128], (((1,), (1,)), ((), ())), preferred_element_type=F32
                ) * scale
                limit = count[h, b] * BLOCK
                live = lax.broadcasted_iota(jnp.int32, (BLOCK, KMAX * BLOCK), 1) < limit
                s = jnp.where(live, s, -jnp.inf)
                raised = jnp.exp(s - jnp.max(s, axis=-1, keepdims=True))
                w = (raised / jnp.sum(raised, axis=-1, keepdims=True)).astype(BF16)
                mixed = jnp.dot(w, both[:, 128:256], preferred_element_type=F32)
                rows = pl.ds(pl.multiple_of(b * BLOCK, BLOCK), BLOCK)
                at[h, x, y, rows, :] = (mixed * sign).astype(BF16)
            return carry

        lax.fori_loop(0, 3, two_blocks, 0)

    def final(h):
        def final_step(i, carry):
            part = jnp.zeros((ROWS, SLICE), F32)
            for u in range(2):
                j = i * 4 + u * 2
                a = jnp.concatenate([at[h, i, u * 2], at[h, i, u * 2 + 1]], axis=-1)
                part = part + jnp.dot(
                    a, wo[h, pl.ds(j, 2)].reshape(256, SLICE), preferred_element_type=F32
                )
            oacc[...] += part
            return carry

        lax.fori_loop(0, 4, final_step, 0)

    oacc[...] = jnp.zeros((ROWS, SLICE), F32)
    wr_[0].step(3)
    wr_[1].step(3)
    wr_[0].step(4)
    wr_[1].step(4)
    wr_[2].step(1)
    wr_[0].finish()
    project(0)
    kr_[0].own()
    wr_[2].step(2)
    wr_[1].finish()
    project(1)
    kr_[1].own()
    wr_[2].step(3)
    kr_[0].step(1)
    wr_[2].step(4)
    kr_[0].step(2)
    wr_[2].finish()
    project(2)
    kr_[0].step(3)
    kr_[1].step(1)
    kr_[2].own()
    kr_[0].step(4)
    kr_[1].step(2)

    wo_own.wait()

    def wo_wait(i, carry):
        wo_copy(i).wait()
        return carry

    lax.fori_loop(1, 16, wo_wait, 0)
    wo_swap = send(wo.at[:, :, half], wo.at[:, :, half], ws.at[0], wr.at[0], partner)

    kr_[0].finish()
    attend(0)
    ax[0].start()
    kr_[1].step(3)
    kr_[2].step(1)
    ax[0].one()
    kr_[1].step(4)
    ax[0].two()
    kr_[2].step(2)
    kr_[1].finish()
    attend(1)
    ax[0].three()
    ax[1].start()
    kr_[2].step(3)
    ax[0].four()
    ax[1].one()
    ax[1].two()
    kr_[2].step(4)
    ax[1].three()
    wo_swap.wait_recv()
    kr_[2].finish()
    attend(2)
    ax[2].start()
    final(0)
    ax[2].one()
    ax[1].four()
    ax[2].two()
    final(1)
    ax[2].three()
    ax[2].four()
    final(2)
    out[...] = oacc[...]
    for cp in started:
        if id(cp) not in drained:
            cp.wait_send()


def per_device(
    hidden_rows,
    gen_weight,
    noise,
    timesteps,
    qkv_weight,
    out_weight,
    qk_gain,
    block_keys,
    block_count,
):
    turn = timesteps.astype(F32) * (math.pi / 2000.0)
    angles = jnp.stack([jnp.cos(turn), jnp.sin(turn)])
    smem = pl.BlockSpec(memory_space=pltpu.SMEM)
    hbm = pl.BlockSpec(memory_space=pl.ANY)
    dma = pltpu.SemaphoreType.DMA
    return pl.pallas_call(
        kernel,
        out_shape=jax.ShapeDtypeStruct((ROWS, SLICE), F32),
        in_specs=[smem] * 4 + [hbm] * 5,
        out_specs=pl.BlockSpec(memory_space=pltpu.VMEM),
        scratch_shapes=[
            pltpu.VMEM((ROWS, D), BF16),
            pltpu.VMEM((D, SLICE), BF16),
            pltpu.VMEM((ROWS, D), BF16),
            pltpu.VMEM((NX, NY, ROWS, SLICE), BF16),
            pltpu.VMEM((HEADS_HERE, NZ, 2, SLICE, ROWS), BF16),
            pltpu.VMEM((HEADS_HERE, 6, BLOCK, HEAD_DIM), BF16),
            *[pltpu.VMEM((NZ, 2, 6, BLOCK, 2 * HEAD_DIM), BF16)] * HEADS_HERE,
            pltpu.VMEM((16, HEADS_HERE, 128, SLICE), BF16),
            pltpu.VMEM((HEADS_HERE, 16, 128, SLICE), BF16),
            pltpu.VMEM((HEADS_HERE, NX, NY, ROWS, HEAD_DIM), BF16),
            pltpu.VMEM((ROWS, ROWS), F32),
            pltpu.VMEM((ROWS, SLICE), F32),
            dma((8,)),
            dma((6, 14)),
            dma((6, 14)),
            dma((6, 8)),
            dma((6, 8)),
            dma((4, 16)),
            dma((4, 16)),
            dma((16,)),
            dma((16,)),
        ],
        compiler_params=pltpu.CompilerParams(
            collective_id=0, has_side_effects=True, vmem_limit_bytes=67043328
        ),
    )(
        angles, qk_gain, block_keys, block_count,
        hidden_rows, gen_weight, noise, qkv_weight, out_weight,
    )


def solution(mesh):
    placed = (
        P("seq", None),
        P(None, ("role", "head")),
        P("seq", None),
        P("seq"),
        P("role", "seq", "head"),
        P("role", "head", None),
        P("role", None, "head"),
        P("head", "seq", None),
        P("head", "seq"),
    )
    return jax.shard_map(
        per_device,
        mesh=mesh,
        in_specs=placed,
        out_specs=P("seq", ("role", "head")),
        check_vma=False,
    )
```

```python
import math

import jax
import jax.numpy as jnp
from jax import lax
from jax.experimental import pallas as pl
from jax.experimental.pallas import tpu as pltpu
from jax.sharding import PartitionSpec as P

HEAD_DIM = 128
BLOCK = 64
KMAX = 8
ROWS = 384
D = 5120
SLICE = 320
NX, NY, NZ = 4, 4, 8
HEADS_HERE = 3
MESH = pl.DeviceIdType.MESH
F32 = jnp.float32
BF16 = jnp.bfloat16


def rms(values):
    return values * lax.rsqrt(jnp.mean(values * values, axis=-1, keepdims=True) + 1e-06)


def kernel(
    steps, gain, keys, count,
    hidden, gen_w, noise, qkv_w, out_w,
    out,
    hid, gw, nz, xg, wb, qt, kv0, kv1, kv2, sl, wo, at, acc, oacc,
    loc_sem, zs, zr, ps, pr, xs, xr, ws, wr,
):
    kv = (kv0, kv1, kv2)
    role = lax.axis_index("role")
    seq = lax.axis_index("seq")
    head = lax.axis_index("head")
    z, c = seq // 2, seq % 2
    x = role * 2 + head // 4
    y = head % 4
    me = x * NY + y

    def at_x(d):
        xx = (x + d + NX) % NX
        return {"role": xx // 2, "head": (xx % 2) * 4 + y}

    def at_y(d):
        return {"head": (head // 4) * 4 + (y + d + NY) % NY}

    def at_z(d):
        return {"seq": ((z + d + NZ) % NZ) * 2 + c}

    def plane(i):
        j = (me + i) % 16
        return {"role": j // 8, "head": j % 8}

    partner = {"seq": z * 2 + 1 - c}

    def local(src, dst, i):
        cp = pltpu.make_async_copy(src, dst, loc_sem.at[i])
        cp.start()
        return cp

    w_own = [
        local(qkv_w.at[0, :, pl.ds(h * ROWS, ROWS)], wb.at[h, z, c], h)
        for h in range(HEADS_HERE)
    ]
    hid_cp = local(hidden, hid, 3)
    gw_cp = local(gen_w, gw, 4)
    nz_cp = local(noise, nz, 5)

    barrier = pltpu.get_barrier_semaphore()
    for d in (1, -1):
        pl.semaphore_signal(barrier, inc=1, device_id=at_z(d), device_id_type=MESH)
    pl.semaphore_signal(barrier, inc=1, device_id=partner, device_id_type=MESH)

    def greet(i, carry):
        pl.semaphore_signal(barrier, inc=1, device_id=plane(i), device_id_type=MESH)
        return carry

    lax.fori_loop(1, 16, greet, 0)
    pl.semaphore_wait(barrier, 18)

    started = []

    def send(src, dst, ssem, rsem, device):
        cp = pltpu.make_async_remote_copy(
            src_ref=src, dst_ref=dst, send_sem=ssem, recv_sem=rsem,
            device_id=device, device_id_type=MESH,
        )
        cp.start()
        started.append(cp)
        return cp

    class Ring:
        def __init__(self, g, part, whole):
            self.g, self.part, self.whole = g, part, whole
            self.cp = {}

        def push(self, way, half, k):
            shard = (z + NZ - way * (k - 1)) % NZ
            i = (0 if way > 0 else 7) + (k - 1 if half == 0 else (4 if way > 0 else 3) + k - 1)
            ref = self.part(shard, half)
            self.cp[way, half, k] = send(
                ref, ref, zs.at[self.g, i], zr.at[self.g, i], at_z(way)
            )

        def give(self, d):
            ref = self.whole((z + d + NZ) % NZ)
            n = d + 3
            self.cp["p", d] = send(ref, ref, ps.at[self.g, n], pr.at[self.g, n], partner)

        def own(self):
            self.push(1, 0, 1)
            self.push(-1, 1, 1)
            self.push(1, 1, 1)
            self.push(-1, 0, 1)
            self.give(0)

        def step_a(self, k):
            for way, half in ((1, 0), (-1, 1)):
                self.cp[way, half, k].wait_recv()
                if k < 4:
                    self.push(way, half, k + 1)
            if k == 4:
                self.give(4)

        def step_b(self, k):
            for way, half in ((1, 1), (-1, 0)):
                self.cp[way, half, k].wait_recv()
                if k < 3:
                    self.push(way, half, k + 1)
            self.give(-k)
            self.give(k)

        def finish(self):
            for d in range(-3, 5):
                self.cp["p", d].wait_recv()

    def w_ring(h):
        return Ring(
            h,
            lambda zz, half: wb.at[h, zz, c, pl.ds(half * 160, 160)],
            lambda zz: wb.at[h, zz, c],
        )

    def kv_ring(h):
        return Ring(
            3 + h,
            lambda zz, half: kv[h].at[zz, c, pl.ds(half * 3, 3)],
            lambda zz: kv[h].at[zz, c],
        )

    class Plane:
        def __init__(self, g, buf):
            self.g, self.buf = g, buf
            self.n = 0
            self.cp = {}

        def push(self, name, ref, device):
            self.cp[name] = send(
                ref, ref, xs.at[self.g, self.n], xr.at[self.g, self.n], device
            )
            self.n += 1

        def start(self):
            b = self.buf
            for d in (1, -1):
                self.push(("a1", d), b.at[x, y, pl.ds(0, 192)], at_x(d))
                self.push(("b1", d), b.at[x, y, pl.ds(192, 192)], at_y(d))

        def one(self):
            b = self.buf
            for n, d in enumerate((1, -1)):
                self.cp["a1", d].wait_recv()
                self.push(("a2", d), b.at[(x - d + NX) % NX, y, pl.ds(n * 96, 96)], at_x(d))
                self.cp["b1", d].wait_recv()
                self.push(("b2", d), b.at[x, (y - d + NY) % NY, pl.ds(192 + n * 96, 96)], at_y(d))

        def two(self):
            b = self.buf
            for d in (1, -1):
                self.cp["a2", d].wait_recv()
            for d in (1, -1):
                self.push(("a3", d), b.at[:, y, pl.ds(0, 192)], at_y(d))
            for d in (1, -1):
                self.cp["b2", d].wait_recv()
            for d in (1, -1):
                self.push(("b3", d), b.at[x, :, pl.ds(192, 192)], at_x(d))

        def three(self):
            b = self.buf
            for n, d in enumerate((1, -1)):
                self.cp["a3", d].wait_recv()
                self.push(
                    ("a4", d), b.at[pl.ds(2 * n, 2), (y - d + NY) % NY, pl.ds(0, 192)], at_y(d)
                )
                self.cp["b3", d].wait_recv()
                self.push(
                    ("b4", d), b.at[(x - d + NX) % NX, pl.ds(2 * n, 2), pl.ds(192, 192)], at_x(d)
                )

        def four(self):
            for d in (1, -1):
                self.cp["a4", d].wait_recv()
                self.cp["b4", d].wait_recv()

    wr_ = [w_ring(h) for h in range(HEADS_HERE)]
    kr_ = [kv_ring(h) for h in range(HEADS_HERE)]
    gx = Plane(0, xg)
    ax = [Plane(1 + h, at.at[h]) for h in range(HEADS_HERE)]

    def gen_step(i, carry):
        k0 = pl.multiple_of(i * 1024, 1024)
        acc[:, :SLICE] += lax.dot_general(
            hid[:, pl.ds(k0, 1024)], gw[:, pl.ds(k0, 1024)],
            (((1,), (1,)), ((), ())), preferred_element_type=F32,
        )
        return carry

    def generate():
        hid_cp.wait()
        gw_cp.wait()
        acc[:, :SLICE] = jnp.zeros((ROWS, SLICE), F32)
        lax.fori_loop(0, D // 1024, gen_step, 0)
        xg[x, y] = acc[:, :SLICE].astype(BF16)
        held.append(local(out_w.at[0], hid, 6))

    def cut():
        held.pop().wait()
        for j in range(16):
            sl[j] = hid[:, j * SLICE:(j + 1) * SLICE].reshape(HEADS_HERE, 128, SLICE)

    half = pl.ds(c * 64, 64)
    wo_own = pltpu.make_async_copy(sl.at[me, :, half], wo.at[:, me, half], loc_sem.at[7])

    def wo_copy(i):
        j = (me + i) % 16
        return pltpu.make_async_remote_copy(
            src_ref=sl.at[j, :, half], dst_ref=wo.at[:, me, half],
            send_sem=ws.at[i], recv_sem=wr.at[i],
            device_id=plane(i), device_id_type=MESH,
        )

    def wo_start(i, carry):
        wo_copy(i).start()
        return carry

    def wo_wait(i, carry):
        wo_copy(i).wait()
        return carry

    def swap_start():
        wo_own.start()
        lax.fori_loop(1, 16, wo_start, 0)

    def swap_end():
        wo_own.wait()
        lax.fori_loop(1, 16, wo_wait, 0)
        held.append(send(wo.at[:, :, half], wo.at[:, :, half], ws.at[0], wr.at[0], partner))

    def norm_step(b, carry):
        rows = pl.ds(pl.multiple_of(b * BLOCK, BLOCK), BLOCK)
        turn = jnp.full((8, SLICE), steps[b], jnp.int32).astype(F32) * (math.pi / 2000.0)
        ca, sa = jnp.cos(turn)[0:1], jnp.sin(turn)[0:1]

        def noisy(j):
            g = xg[j // NY, j % NY, rows, :].astype(F32)
            n = nz[rows, j * SLICE:(j + 1) * SLICE].astype(F32)
            return ca * g + sa * n

        total = jnp.zeros((BLOCK, 1), F32)
        for j in range(16):
            v = noisy(j)
            total = total + jnp.sum(v * v, axis=-1, keepdims=True)
        inv = lax.rsqrt(total * (1.0 / D) + 1e-06)
        for j in range(16):
            xg[j // NY, j % NY, rows, :] = (noisy(j) * inv).astype(BF16)
        return carry

    def norm():
        nz_cp.wait()
        for cp in gx.cp.values():
            cp.wait_send()
        lax.fori_loop(0, ROWS // BLOCK, norm_step, 0)

    def project(h):
        acc[...] = jnp.zeros((ROWS, ROWS), F32)

        def proj_step(zz, carry):
            part = jnp.zeros((ROWS, ROWS), F32)
            for cc in range(2):
                s = zz * 2 + cc
                part = part + jnp.dot(
                    xg[s // NY, s % NY], wb[h, zz, cc], preferred_element_type=F32
                )
            acc[...] += part
            return carry

        lax.fori_loop(0, NZ, proj_step, 0)
        q = (rms(acc[:, 0:128]) * gain[0, 0, h]).astype(BF16)
        k = (rms(acc[:, 128:256]) * gain[0, 1, h]).astype(BF16)
        v = acc[:, 256:384].astype(BF16)
        qt[h] = q.reshape(6, BLOCK, HEAD_DIM)
        kv[h][z, c, :, :, 0:128] = k.reshape(6, BLOCK, HEAD_DIM)
        kv[h][z, c, :, :, 128:256] = v.reshape(6, BLOCK, HEAD_DIM)

    sign = (2 * role - 1).astype(F32)
    scale = 1.0 / math.sqrt(HEAD_DIM)

    def attend(h):
        def two_blocks(b2, carry):
            for u in range(2):
                b = b2 * 2 + u
                q = qt[h, b]
                got = []
                for j in range(KMAX):
                    kb = keys[h, b, j]
                    s = kb // 6
                    got.append(kv[h][s // 2, s % 2, kb - s * 6])
                both = jnp.concatenate(got, axis=0)
                s = lax.dot_general(
                    q, both[:, 0:128], (((1,), (1,)), ((), ())), preferred_element_type=F32
                ) * scale
                limit = count[h, b] * BLOCK
                live = lax.broadcasted_iota(jnp.int32, (BLOCK, KMAX * BLOCK), 1) < limit
                s = jnp.where(live, s, -jnp.inf)
                raised = jnp.exp(s - jnp.max(s, axis=-1, keepdims=True))
                w = (raised / jnp.sum(raised, axis=-1, keepdims=True)).astype(BF16)
                mixed = jnp.dot(w, both[:, 128:256], preferred_element_type=F32)
                rows = pl.ds(pl.multiple_of(b * BLOCK, BLOCK), BLOCK)
                at[h, x, y, rows, :] = (mixed * sign).astype(BF16)
            return carry

        lax.fori_loop(0, 3, two_blocks, 0)

    def final(h):
        def final_step(i, carry):
            part = jnp.zeros((ROWS, SLICE), F32)
            for u in range(2):
                j = i * 4 + u * 2
                a = jnp.concatenate([at[h, i, u * 2], at[h, i, u * 2 + 1]], axis=-1)
                part = part + jnp.dot(
                    a, wo[h, pl.ds(j, 2)].reshape(256, SLICE), preferred_element_type=F32
                )
            oacc[...] += part
            return carry

        lax.fori_loop(0, 4, final_step, 0)

    held = []
    for h in range(HEADS_HERE):
        w_own[h].wait()
    oacc[...] = jnp.zeros((ROWS, SLICE), F32)
    wr_[0].own()
    generate()
    gx.start()
    cut()
    wr_[0].step_a(1)
    wr_[0].step_b(1)
    wr_[1].own()
    gx.one()
    wr_[0].step_a(2)
    gx.two()
    wr_[0].step_b(2)
    wr_[1].step_a(1)
    wr_[1].step_b(1)
    wr_[0].step_a(3)
    wr_[0].step_b(3)
    wr_[2].own()
    wr_[1].step_a(2)
    gx.three()
    wr_[1].step_b(2)
    wr_[0].step_a(4)
    wr_[2].step_a(1)
    wr_[0].finish()
    gx.four()
    norm()
    wr_[1].step_a(3)
    wr_[1].step_b(3)
    wr_[2].step_b(1)
    project(0)
    wr_[2].step_a(2)
    kr_[0].own()
    swap_start()
    wr_[1].step_a(4)
    wr_[2].step_b(2)
    wr_[2].step_a(3)
    wr_[1].finish()
    project(1)
    kr_[0].step_a(1)
    kr_[0].step_b(1)
    kr_[1].own()
    wr_[2].step_b(3)
    wr_[2].step_a(4)
    kr_[0].step_a(2)
    kr_[0].step_b(2)
    kr_[1].step_a(1)
    wr_[2].finish()
    project(2)
    kr_[0].step_a(3)
    kr_[1].step_b(1)
    kr_[2].own()
    kr_[0].step_b(3)
    kr_[1].step_a(2)
    kr_[0].step_a(4)
    kr_[1].step_b(2)
    kr_[0].finish()
    attend(0)
    kr_[2].step_a(1)
    kr_[2].step_b(1)
    ax[0].start()
    kr_[1].step_a(3)
    swap_end()
    ax[0].one()
    kr_[1].step_b(3)
    ax[0].two()
    kr_[2].step_a(2)
    kr_[2].step_b(2)
    kr_[1].step_a(4)
    kr_[2].step_a(3)
    ax[0].three()
    kr_[2].step_b(3)
    kr_[2].step_a(4)
    ax[0].four()
    held.pop().wait_recv()
    final(0)
    kr_[1].finish()
    attend(1)
    ax[1].start()
    kr_[2].finish()
    attend(2)
    ax[2].start()
    ax[1].one()
    ax[2].one()
    ax[1].two()
    ax[2].two()
    ax[1].three()
    ax[2].three()
    ax[1].four()
    final(1)
    ax[2].four()
    final(2)
    out[...] = oacc[...].T
    drained = {id(cp) for cp in gx.cp.values()}
    for cp in started:
        if id(cp) not in drained:
            cp.wait_send()


def per_device(
    hidden_rows,
    gen_weight,
    noise,
    timesteps,
    qkv_weight,
    out_weight,
    qk_gain,
    block_keys,
    block_count,
):
    smem = pl.BlockSpec(memory_space=pltpu.SMEM)
    hbm = pl.BlockSpec(memory_space=pl.ANY)
    dma = pltpu.SemaphoreType.DMA
    return pl.pallas_call(
        kernel,
        out_shape=jax.ShapeDtypeStruct((SLICE, ROWS), F32),
        in_specs=[smem] * 4 + [hbm] * 5,
        out_specs=pl.BlockSpec(memory_space=pltpu.VMEM),
        scratch_shapes=[
            pltpu.VMEM((ROWS, D), BF16),
            pltpu.VMEM((SLICE, D), BF16),
            pltpu.VMEM((ROWS, D), BF16),
            pltpu.VMEM((NX, NY, ROWS, SLICE), BF16),
            pltpu.VMEM((HEADS_HERE, NZ, 2, SLICE, ROWS), BF16),
            pltpu.VMEM((HEADS_HERE, 6, BLOCK, HEAD_DIM), BF16),
            *[pltpu.VMEM((NZ, 2, 6, BLOCK, 2 * HEAD_DIM), BF16)] * HEADS_HERE,
            pltpu.VMEM((16, HEADS_HERE, 128, SLICE), BF16),
            pltpu.VMEM((HEADS_HERE, 16, 128, SLICE), BF16),
            pltpu.VMEM((HEADS_HERE, NX, NY, ROWS, HEAD_DIM), BF16),
            pltpu.VMEM((ROWS, ROWS), F32),
            pltpu.VMEM((ROWS, SLICE), F32),
            dma((8,)),
            dma((6, 14)),
            dma((6, 14)),
            dma((6, 8)),
            dma((6, 8)),
            dma((4, 16)),
            dma((4, 16)),
            dma((16,)),
            dma((16,)),
        ],
        compiler_params=pltpu.CompilerParams(
            collective_id=0, has_side_effects=True, vmem_limit_bytes=67043328
        ),
    )(
        timesteps, qk_gain, block_keys, block_count,
        hidden_rows, gen_weight.T, noise, qkv_weight, out_weight,
    ).T


def solution(mesh):
    placed = (
        P("seq", None),
        P(None, ("role", "head")),
        P("seq", None),
        P("seq"),
        P("role", "seq", "head"),
        P("role", "head", None),
        P("role", None, "head"),
        P("head", "seq", None),
        P("head", "seq"),
    )
    return jax.shard_map(
        per_device,
        mesh=mesh,
        in_specs=placed,
        out_specs=P("seq", ("role", "head")),
        check_vma=False,
    )
```

```python
import math

import jax
import jax.numpy as jnp
from jax import lax
from jax.experimental import pallas as pl
from jax.experimental.pallas import tpu as pltpu
from jax.sharding import PartitionSpec as P

HEAD_DIM = 128
BLOCK = 64
KMAX = 8
ROWS = 384
D = 5120
SLICE = 320
NX, NY, NZ = 4, 4, 8
HEADS_HERE = 3
MESH = pl.DeviceIdType.MESH
F32 = jnp.float32
BF16 = jnp.bfloat16


def rms(values):
    return values * lax.rsqrt(jnp.mean(values * values, axis=-1, keepdims=True) + 1e-06)


def kernel(
    steps, gain, keys, count,
    hidden, gen_w, noise, qkv_w, out_w,
    out,
    hid, gw, nz, xg, wb, qt, kv0, kv1, kv2, sl, wo, at, acc, oacc,
    loc_sem, zs, zr, ps, pr, xs, xr, ws, wr,
):
    kv = (kv0, kv1, kv2)
    role = lax.axis_index("role")
    seq = lax.axis_index("seq")
    head = lax.axis_index("head")
    z, c = seq // 2, seq % 2
    x = role * 2 + head // 4
    y = head % 4
    me = x * NY + y

    def at_x(d):
        xx = (x + d + NX) % NX
        return {"role": xx // 2, "head": (xx % 2) * 4 + y}

    def at_y(d):
        return {"head": (head // 4) * 4 + (y + d + NY) % NY}

    def at_z(d):
        return {"seq": ((z + d + NZ) % NZ) * 2 + c}

    def plane(i):
        j = (me + i) % 16
        return {"role": j // 8, "head": j % 8}

    partner = {"seq": z * 2 + 1 - c}

    barrier = pltpu.get_barrier_semaphore()
    near = [at_z(1), at_z(-1), partner, at_x(1), at_x(-1), at_y(1), at_y(-1)]
    for device in near:
        pl.semaphore_signal(barrier, inc=1, device_id=device, device_id_type=MESH)

    def local(src, dst, i):
        cp = pltpu.make_async_copy(src, dst, loc_sem.at[i])
        cp.start()
        return cp

    w_own = [
        local(qkv_w.at[0, :, pl.ds(h * ROWS, ROWS)], wb.at[h, z, c], h)
        for h in range(HEADS_HERE)
    ]
    hid_cp = local(hidden, hid, 3)
    gw_cp = local(gen_w, gw, 4)
    nz_cp = local(noise, nz, 5)

    pl.semaphore_wait(barrier, len(near))

    started = []

    def send(src, dst, ssem, rsem, device):
        cp = pltpu.make_async_remote_copy(
            src_ref=src, dst_ref=dst, send_sem=ssem, recv_sem=rsem,
            device_id=device, device_id_type=MESH,
        )
        cp.start()
        started.append(cp)
        return cp

    class Ring:
        def __init__(self, g, part, whole, own_part, own_whole):
            self.g, self.part, self.whole = g, part, whole
            self.own_part, self.own_whole = own_part, own_whole
            self.cp = {}

        def push(self, way, half, k):
            shard = (z + NZ - way * (k - 1)) % NZ
            i = (0 if way > 0 else 7) + (k - 1 if half == 0 else (4 if way > 0 else 3) + k - 1)
            ref = self.part(shard, half)
            src = self.own_part(half) if k == 1 else ref
            self.cp[way, half, k] = send(
                src, ref, zs.at[self.g, i], zr.at[self.g, i], at_z(way)
            )

        def give(self, d):
            ref = self.whole((z + d + NZ) % NZ)
            n = d + 3
            src = self.own_whole() if d == 0 else ref
            self.cp["p", d] = send(src, ref, ps.at[self.g, n], pr.at[self.g, n], partner)

        def own(self):
            self.push(1, 0, 1)
            self.push(-1, 1, 1)
            self.push(1, 1, 1)
            self.push(-1, 0, 1)
            self.give(0)

        def step_a(self, k):
            for way, half in ((1, 0), (-1, 1)):
                self.cp[way, half, k].wait_recv()
                if k < 4:
                    self.push(way, half, k + 1)
            if k == 4:
                self.give(4)

        def step_b(self, k):
            for way, half in ((1, 1), (-1, 0)):
                self.cp[way, half, k].wait_recv()
                if k < 3:
                    self.push(way, half, k + 1)
            self.give(-k)
            self.give(k)

        def finish(self):
            for d in range(-3, 5):
                self.cp["p", d].wait_recv()

    def w_ring(h):
        return Ring(
            h,
            lambda zz, half: wb.at[h, zz, c, pl.ds(half * 160, 160)],
            lambda zz: wb.at[h, zz, c],
            lambda half: qkv_w.at[0, pl.ds(half * 160, 160), pl.ds(h * ROWS, ROWS)],
            lambda: qkv_w.at[0, :, pl.ds(h * ROWS, ROWS)],
        )

    def kv_ring(h):
        return Ring(
            3 + h,
            lambda zz, half: kv[h].at[zz, c, pl.ds(half * 3, 3)],
            lambda zz: kv[h].at[zz, c],
            lambda half: kv[h].at[z, c, pl.ds(half * 3, 3)],
            lambda: kv[h].at[z, c],
        )

    class Plane:
        def __init__(self, g, buf):
            self.g, self.buf = g, buf
            self.n = 0
            self.cp = {}

        def push(self, name, ref, device):
            self.cp[name] = send(
                ref, ref, xs.at[self.g, self.n], xr.at[self.g, self.n], device
            )
            self.n += 1

        def start(self):
            b = self.buf
            for d in (1, -1):
                self.push(("a1", d), b.at[x, y, pl.ds(0, 192)], at_x(d))
                self.push(("b1", d), b.at[x, y, pl.ds(192, 192)], at_y(d))

        def one(self):
            b = self.buf
            for n, d in enumerate((1, -1)):
                self.cp["a1", d].wait_recv()
                self.push(("a2", d), b.at[(x - d + NX) % NX, y, pl.ds(n * 96, 96)], at_x(d))
                self.cp["b1", d].wait_recv()
                self.push(("b2", d), b.at[x, (y - d + NY) % NY, pl.ds(192 + n * 96, 96)], at_y(d))

        def two(self):
            b = self.buf
            for d in (1, -1):
                self.cp["a2", d].wait_recv()
            for d in (1, -1):
                self.push(("a3", d), b.at[:, y, pl.ds(0, 192)], at_y(d))
            for d in (1, -1):
                self.cp["b2", d].wait_recv()
            for d in (1, -1):
                self.push(("b3", d), b.at[x, :, pl.ds(192, 192)], at_x(d))

        def three(self):
            b = self.buf
            for n, d in enumerate((1, -1)):
                self.cp["a3", d].wait_recv()
                self.push(
                    ("a4", d), b.at[pl.ds(2 * n, 2), (y - d + NY) % NY, pl.ds(0, 192)], at_y(d)
                )
                self.cp["b3", d].wait_recv()
                self.push(
                    ("b4", d), b.at[(x - d + NX) % NX, pl.ds(2 * n, 2), pl.ds(192, 192)], at_x(d)
                )

        def four(self):
            for d in (1, -1):
                self.cp["a4", d].wait_recv()
                self.cp["b4", d].wait_recv()

    wr_ = [w_ring(h) for h in range(HEADS_HERE)]
    kr_ = [kv_ring(h) for h in range(HEADS_HERE)]
    gx = Plane(0, xg)
    ax = [Plane(1 + h, at.at[h]) for h in range(HEADS_HERE)]

    def gen_step(i, carry):
        k0 = pl.multiple_of(i * 1024, 1024)
        acc[:, :SLICE] += lax.dot_general(
            hid[:, pl.ds(k0, 1024)], gw[:, pl.ds(k0, 1024)],
            (((1,), (1,)), ((), ())), preferred_element_type=F32,
        )
        return carry

    def generate():
        hid_cp.wait()
        gw_cp.wait()
        acc[:, :SLICE] = jnp.zeros((ROWS, SLICE), F32)
        lax.fori_loop(0, D // 1024, gen_step, 0)
        xg[x, y] = acc[:, :SLICE].astype(BF16)
        held.append(local(out_w.at[0], hid, 6))

    def cut():
        held.pop().wait()
        for j in range(16):
            sl[j] = hid[:, j * SLICE:(j + 1) * SLICE].reshape(HEADS_HERE, 128, SLICE)

    half = pl.ds(c * 64, 64)
    wo_own = pltpu.make_async_copy(sl.at[me, :, half], wo.at[:, me, half], loc_sem.at[7])

    def wo_copy(i):
        j = (me + i) % 16
        return pltpu.make_async_remote_copy(
            src_ref=sl.at[j, :, half], dst_ref=wo.at[:, me, half],
            send_sem=ws.at[i], recv_sem=wr.at[i],
            device_id=plane(i), device_id_type=MESH,
        )

    def wo_start(i, carry):
        wo_copy(i).start()
        return carry

    def wo_wait(i, carry):
        wo_copy(i).wait()
        return carry

    def swap_start():
        wo_own.start()
        lax.fori_loop(1, 16, wo_start, 0)

    def swap_end():
        wo_own.wait()
        lax.fori_loop(1, 16, wo_wait, 0)
        held.append(send(wo.at[:, :, half], wo.at[:, :, half], ws.at[0], wr.at[0], partner))

    def norm_step(b, carry):
        rows = pl.ds(pl.multiple_of(b * BLOCK, BLOCK), BLOCK)
        turn = jnp.full((8, SLICE), steps[b], jnp.int32).astype(F32) * (math.pi / 2000.0)
        ca, sa = jnp.cos(turn)[0:1], jnp.sin(turn)[0:1]

        def noisy(j):
            g = xg[j // NY, j % NY, rows, :].astype(F32)
            n = nz[rows, j * SLICE:(j + 1) * SLICE].astype(F32)
            return ca * g + sa * n

        total = jnp.zeros((BLOCK, 1), F32)
        for j in range(16):
            v = noisy(j)
            total = total + jnp.sum(v * v, axis=-1, keepdims=True)
        inv = lax.rsqrt(total * (1.0 / D) + 1e-06)
        for j in range(16):
            xg[j // NY, j % NY, rows, :] = (noisy(j) * inv).astype(BF16)
        return carry

    def norm():
        nz_cp.wait()
        for cp in gx.cp.values():
            cp.wait_send()
        lax.fori_loop(0, ROWS // BLOCK, norm_step, 0)

    def project(h):
        w_own[h].wait()
        acc[...] = jnp.zeros((ROWS, ROWS), F32)

        def proj_step(zz, carry):
            part = jnp.zeros((ROWS, ROWS), F32)
            for cc in range(2):
                s = zz * 2 + cc
                part = part + jnp.dot(
                    xg[s // NY, s % NY], wb[h, zz, cc], preferred_element_type=F32
                )
            acc[...] += part
            return carry

        lax.fori_loop(0, NZ, proj_step, 0)
        q = (rms(acc[:, 0:128]) * gain[0, 0, h]).astype(BF16)
        k = (rms(acc[:, 128:256]) * gain[0, 1, h]).astype(BF16)
        v = acc[:, 256:384].astype(BF16)
        qt[h] = q.reshape(6, BLOCK, HEAD_DIM)
        kv[h][z, c, :, :, 0:128] = k.reshape(6, BLOCK, HEAD_DIM)
        kv[h][z, c, :, :, 128:256] = v.reshape(6, BLOCK, HEAD_DIM)

    sign = (2 * role - 1).astype(F32)
    scale = 1.0 / math.sqrt(HEAD_DIM)

    def attend(h):
        def two_blocks(b2, carry):
            for u in range(2):
                b = b2 * 2 + u
                q = qt[h, b]
                got = []
                for j in range(KMAX):
                    kb = keys[h, b, j]
                    s = kb // 6
                    got.append(kv[h][s // 2, s % 2, kb - s * 6])
                both = jnp.concatenate(got, axis=0)
                s = lax.dot_general(
                    q, both[:, 0:128], (((1,), (1,)), ((), ())), preferred_element_type=F32
                ) * scale
                limit = count[h, b] * BLOCK
                live = lax.broadcasted_iota(jnp.int32, (BLOCK, KMAX * BLOCK), 1) < limit
                s = jnp.where(live, s, -jnp.inf)
                raised = jnp.exp(s - jnp.max(s, axis=-1, keepdims=True))
                w = (raised / jnp.sum(raised, axis=-1, keepdims=True)).astype(BF16)
                mixed = jnp.dot(w, both[:, 128:256], preferred_element_type=F32)
                rows = pl.ds(pl.multiple_of(b * BLOCK, BLOCK), BLOCK)
                at[h, x, y, rows, :] = (mixed * sign).astype(BF16)
            return carry

        lax.fori_loop(0, 3, two_blocks, 0)

    def final(h):
        def final_step(i, carry):
            part = jnp.zeros((ROWS, SLICE), F32)
            for u in range(2):
                j = i * 4 + u * 2
                a = jnp.concatenate([at[h, i, u * 2], at[h, i, u * 2 + 1]], axis=-1)
                part = part + jnp.dot(
                    a, wo[h, pl.ds(j, 2)].reshape(256, SLICE), preferred_element_type=F32
                )
            oacc[...] += part
            return carry

        lax.fori_loop(0, 4, final_step, 0)

    held = []
    oacc[...] = jnp.zeros((ROWS, SLICE), F32)
    wr_[0].own()
    wr_[0].step_a(1)
    wr_[1].own()
    generate()
    gx.start()
    wr_[0].step_b(1)
    cut()
    wr_[0].step_a(2)
    wr_[1].step_a(1)
    gx.one()
    wr_[1].step_b(1)
    gx.two()
    wr_[0].step_b(2)
    wr_[0].step_a(3)
    wr_[2].own()
    wr_[1].step_a(2)
    wr_[1].step_b(2)
    wr_[0].step_b(3)
    gx.three()
    wr_[0].step_a(4)
    wr_[2].step_a(1)
    wr_[0].finish()
    wr_[2].step_b(1)
    gx.four()
    norm()
    wr_[1].step_a(3)
    wr_[1].step_b(3)
    swap_start()
    wr_[2].step_a(2)
    project(0)
    kr_[0].own()
    wr_[2].step_b(2)
    wr_[1].step_a(4)
    wr_[2].step_a(3)
    kr_[0].step_a(1)
    kr_[0].step_b(1)
    wr_[1].finish()
    project(1)
    wr_[2].step_a(4)
    kr_[1].own()
    wr_[2].step_b(3)
    kr_[0].step_a(2)
    kr_[0].step_b(2)
    kr_[1].step_a(1)
    kr_[1].step_b(1)
    wr_[2].finish()
    project(2)
    kr_[2].own()
    kr_[0].step_a(3)
    kr_[0].step_b(3)
    kr_[1].step_a(2)
    kr_[1].step_b(2)
    kr_[2].step_a(1)
    kr_[2].step_b(1)
    kr_[0].step_a(4)
    swap_end()
    kr_[1].step_a(3)
    kr_[0].finish()
    attend(0)
    kr_[1].step_b(3)
    ax[0].start()
    kr_[2].step_a(2)
    kr_[2].step_b(2)
    ax[0].one()
    kr_[1].step_a(4)
    kr_[2].step_a(3)
    ax[0].two()
    kr_[2].step_b(3)
    kr_[2].step_a(4)
    kr_[1].finish()
    attend(1)
    ax[1].start()
    ax[0].three()
    kr_[2].finish()
    attend(2)
    ax[2].start()
    ax[1].one()
    ax[0].four()
    held.pop().wait_recv()
    final(0)
    ax[2].one()
    ax[1].two()
    ax[2].two()
    ax[1].three()
    ax[2].three()
    ax[1].four()
    final(1)
    ax[2].four()
    final(2)
    out[...] = oacc[...].T
    drained = {id(cp) for cp in gx.cp.values()}
    for cp in started:
        if id(cp) not in drained:
            cp.wait_send()


def per_device(
    hidden_rows,
    gen_weight,
    noise,
    timesteps,
    qkv_weight,
    out_weight,
    qk_gain,
    block_keys,
    block_count,
):
    smem = pl.BlockSpec(memory_space=pltpu.SMEM)
    hbm = pl.BlockSpec(memory_space=pl.ANY)
    dma = pltpu.SemaphoreType.DMA
    return pl.pallas_call(
        kernel,
        out_shape=jax.ShapeDtypeStruct((SLICE, ROWS), F32),
        in_specs=[smem] * 4 + [hbm] * 5,
        out_specs=pl.BlockSpec(memory_space=pltpu.VMEM),
        scratch_shapes=[
            pltpu.VMEM((ROWS, D), BF16),
            pltpu.VMEM((SLICE, D), BF16),
            pltpu.VMEM((ROWS, D), BF16),
            pltpu.VMEM((NX, NY, ROWS, SLICE), BF16),
            pltpu.VMEM((HEADS_HERE, NZ, 2, SLICE, ROWS), BF16),
            pltpu.VMEM((HEADS_HERE, 6, BLOCK, HEAD_DIM), BF16),
            *[pltpu.VMEM((NZ, 2, 6, BLOCK, 2 * HEAD_DIM), BF16)] * HEADS_HERE,
            pltpu.VMEM((16, HEADS_HERE, 128, SLICE), BF16),
            pltpu.VMEM((HEADS_HERE, 16, 128, SLICE), BF16),
            pltpu.VMEM((HEADS_HERE, NX, NY, ROWS, HEAD_DIM), BF16),
            pltpu.VMEM((ROWS, ROWS), F32),
            pltpu.VMEM((ROWS, SLICE), F32),
            dma((8,)),
            dma((6, 14)),
            dma((6, 14)),
            dma((6, 8)),
            dma((6, 8)),
            dma((4, 16)),
            dma((4, 16)),
            dma((16,)),
            dma((16,)),
        ],
        compiler_params=pltpu.CompilerParams(
            collective_id=0, has_side_effects=True, vmem_limit_bytes=67043328
        ),
    )(
        timesteps, qk_gain, block_keys, block_count,
        hidden_rows, gen_weight.T, noise, qkv_weight, out_weight,
    ).T


def solution(mesh):
    placed = (
        P("seq", None),
        P(None, ("role", "head")),
        P("seq", None),
        P("seq"),
        P("role", "seq", "head"),
        P("role", "head", None),
        P("role", None, "head"),
        P("head", "seq", None),
        P("head", "seq"),
    )
    return jax.shard_map(
        per_device,
        mesh=mesh,
        in_specs=placed,
        out_specs=P("seq", ("role", "head")),
        check_vma=False,
    )
```

```python
import math

import jax
import jax.numpy as jnp
from jax import lax
from jax.experimental import pallas as pl
from jax.experimental.pallas import tpu as pltpu
from jax.sharding import PartitionSpec as P

HEAD_DIM = 128
BLOCK = 64
KMAX = 8
ROWS = 384
D = 5120
SLICE = 320
NX, NY, NZ = 4, 4, 8
HEADS_HERE = 3
MESH = pl.DeviceIdType.MESH
F32 = jnp.float32
BF16 = jnp.bfloat16


def rms(values):
    return values * lax.rsqrt(jnp.mean(values * values, axis=-1, keepdims=True) + 1e-06)


def kernel(
    steps, gain, keys, count,
    hidden, gen_w, noise, qkv_w, out_w,
    out,
    hid, gw, nz, xg, wb, qt, kv0, kv1, kv2, sl, wo, at, acc, oacc,
    loc_sem, zs, zr, ps, pr, xs, xr, ws, wr,
):
    kv = (kv0, kv1, kv2)
    role = lax.axis_index("role")
    seq = lax.axis_index("seq")
    head = lax.axis_index("head")
    z, c = seq // 2, seq % 2
    x = role * 2 + head // 4
    y = head % 4
    me = x * NY + y

    def at_x(d):
        xx = (x + d + NX) % NX
        return {"role": xx // 2, "head": (xx % 2) * 4 + y}

    def at_y(d):
        return {"head": (head // 4) * 4 + (y + d + NY) % NY}

    def at_z(d, core=c):
        return {"seq": ((z + d + NZ) % NZ) * 2 + core}

    def plane(i):
        j = (me + i) % 16
        return {"role": j // 8, "head": j % 8}

    partner = {"seq": z * 2 + 1 - c}

    barrier = pltpu.get_barrier_semaphore()
    near = [at_z(1), at_z(-1), partner, at_x(1), at_x(-1), at_y(1), at_y(-1)]
    for device in near:
        pl.semaphore_signal(barrier, inc=1, device_id=device, device_id_type=MESH)

    def local(src, dst, i):
        cp = pltpu.make_async_copy(src, dst, loc_sem.at[i])
        cp.start()
        return cp

    w_own = [
        local(qkv_w.at[0, :, pl.ds(h * ROWS, ROWS)], wb.at[h, z, c], h)
        for h in range(HEADS_HERE)
    ]
    hid_cp = local(hidden, hid, 3)
    gw_cp = local(gen_w, gw, 4)
    nz_cp = local(noise, nz, 5)

    pl.semaphore_wait(barrier, len(near))

    started = []

    def send(src, dst, ssem, rsem, device):
        cp = pltpu.make_async_remote_copy(
            src_ref=src, dst_ref=dst, send_sem=ssem, recv_sem=rsem,
            device_id=device, device_id_type=MESH,
        )
        cp.start()
        started.append(cp)
        return cp

    class Ring:
        def __init__(self, g, part, whole, own_part, own_whole):
            self.g, self.part, self.whole = g, part, whole
            self.own_part, self.own_whole = own_part, own_whole
            self.cp = {}

        def push(self, way, half, k):
            shard = (z + NZ - way * (k - 1)) % NZ
            i = (0 if way > 0 else 7) + (k - 1 if half == 0 else (4 if way > 0 else 3) + k - 1)
            ref = self.part(shard, half)
            src = self.own_part(half) if k == 1 else ref
            self.cp[way, half, k] = send(
                src, ref, zs.at[self.g, i], zr.at[self.g, i], at_z(way)
            )
            if k == 4 and self.g == 5:
                n = 7 if way > 0 else 8
                self.cp["p", 4, half] = send(
                    ref, ref, ps.at[self.g, n], pr.at[self.g, n], at_z(way, 1 - c)
                )

        def give(self, d):
            ref = self.whole((z + d + NZ) % NZ)
            n = d + 3
            src = self.own_whole() if d == 0 else ref
            self.cp["p", d] = send(src, ref, ps.at[self.g, n], pr.at[self.g, n], partner)

        def own(self):
            self.push(1, 0, 1)
            self.push(-1, 1, 1)
            self.push(1, 1, 1)
            self.push(-1, 0, 1)
            self.give(0)

        def step_a(self, k):
            for way, half in ((1, 0), (-1, 1)):
                self.cp[way, half, k].wait_recv()
                if k < 4:
                    self.push(way, half, k + 1)
            if k == 4 and self.g < 5:
                self.give(4)

        def step_b(self, k):
            for way, half in ((1, 1), (-1, 0)):
                self.cp[way, half, k].wait_recv()
                if k < 3:
                    self.push(way, half, k + 1)
            self.give(-k)
            self.give(k)

        def finish(self):
            for d in range(-3, 4):
                self.cp["p", d].wait_recv()
            for key in (("p", 4),) if self.g < 5 else (("p", 4, 0), ("p", 4, 1)):
                self.cp[key].wait_recv()

    def w_ring(h):
        return Ring(
            h,
            lambda zz, half: wb.at[h, zz, c, pl.ds(half * 160, 160)],
            lambda zz: wb.at[h, zz, c],
            lambda half: qkv_w.at[0, pl.ds(half * 160, 160), pl.ds(h * ROWS, ROWS)],
            lambda: qkv_w.at[0, :, pl.ds(h * ROWS, ROWS)],
        )

    def kv_ring(h):
        return Ring(
            3 + h,
            lambda zz, half: kv[h].at[zz, c, pl.ds(half * 3, 3)],
            lambda zz: kv[h].at[zz, c],
            lambda half: kv[h].at[z, c, pl.ds(half * 3, 3)],
            lambda: kv[h].at[z, c],
        )

    class Plane:
        def __init__(self, g, buf):
            self.g, self.buf = g, buf
            self.n = 0
            self.cp = {}

        def push(self, name, ref, device):
            self.cp[name] = send(
                ref, ref, xs.at[self.g, self.n], xr.at[self.g, self.n], device
            )
            self.n += 1

        def start(self):
            b = self.buf
            for d in (1, -1):
                self.push(("a1", d), b.at[x, y, pl.ds(0, 192)], at_x(d))
                self.push(("b1", d), b.at[x, y, pl.ds(192, 192)], at_y(d))

        def one(self):
            b = self.buf
            for n, d in enumerate((1, -1)):
                self.cp["a1", d].wait_recv()
                self.push(("a2", d), b.at[(x - d + NX) % NX, y, pl.ds(n * 96, 96)], at_x(d))
                self.cp["b1", d].wait_recv()
                self.push(("b2", d), b.at[x, (y - d + NY) % NY, pl.ds(192 + n * 96, 96)], at_y(d))

        def two(self):
            b = self.buf
            for d in (1, -1):
                self.cp["a2", d].wait_recv()
            for n in (0, 1):
                for d, m in ((1, n), (-1, 1 - n)):
                    self.push(("a3", d, n), b.at[pl.ds(2 * m, 2), y, pl.ds(0, 192)], at_y(d))
            for d in (1, -1):
                self.cp["b2", d].wait_recv()
            for n in (0, 1):
                for d, m in ((1, n), (-1, 1 - n)):
                    self.push(("b3", d, n), b.at[x, pl.ds(2 * m, 2), pl.ds(192, 192)], at_x(d))

        def three(self):
            b = self.buf
            for n, d in enumerate((1, -1)):
                self.cp["a3", d, 0].wait_recv()
                self.push(
                    ("a4", d), b.at[pl.ds(2 * n, 2), (y - d + NY) % NY, pl.ds(0, 192)], at_y(d)
                )
                self.cp["b3", d, 0].wait_recv()
                self.push(
                    ("b4", d), b.at[(x - d + NX) % NX, pl.ds(2 * n, 2), pl.ds(192, 192)], at_x(d)
                )

        def four(self):
            for d in (1, -1):
                self.cp["a3", d, 1].wait_recv()
                self.cp["b3", d, 1].wait_recv()
                self.cp["a4", d].wait_recv()
                self.cp["b4", d].wait_recv()

    wr_ = [w_ring(h) for h in range(HEADS_HERE)]
    kr_ = [kv_ring(h) for h in range(HEADS_HERE)]
    gx = Plane(0, xg)
    ax = [Plane(1 + h, at.at[h]) for h in range(HEADS_HERE)]

    def gen_step(i, carry):
        k0 = pl.multiple_of(i * 1024, 1024)
        acc[:, :SLICE] += lax.dot_general(
            hid[:, pl.ds(k0, 1024)], gw[:, pl.ds(k0, 1024)],
            (((1,), (1,)), ((), ())), preferred_element_type=F32,
        )
        return carry

    def generate():
        hid_cp.wait()
        gw_cp.wait()
        acc[:, :SLICE] = jnp.zeros((ROWS, SLICE), F32)
        lax.fori_loop(0, D // 1024, gen_step, 0)
        xg[x, y] = acc[:, :SLICE].astype(BF16)
        held.append(local(out_w.at[0], hid, 6))

    def cut():
        held.pop().wait()
        for j in range(16):
            sl[j] = hid[:, j * SLICE:(j + 1) * SLICE].reshape(HEADS_HERE, 128, SLICE)

    half = pl.ds(c * 64, 64)
    wo_own = pltpu.make_async_copy(sl.at[me, :, half], wo.at[:, me, half], loc_sem.at[7])

    def wo_copy(i):
        j = (me + i) % 16
        return pltpu.make_async_remote_copy(
            src_ref=sl.at[j, :, half], dst_ref=wo.at[:, me, half],
            send_sem=ws.at[i], recv_sem=wr.at[i],
            device_id=plane(i), device_id_type=MESH,
        )

    def wo_start(i, carry):
        wo_copy(i).start()
        return carry

    def wo_wait(i, carry):
        wo_copy(i).wait()
        return carry

    def swap_start():
        wo_own.start()
        lax.fori_loop(1, 16, wo_start, 0)

    def swap_end():
        wo_own.wait()
        lax.fori_loop(1, 16, wo_wait, 0)
        held.append(send(wo.at[:, :, half], wo.at[:, :, half], ws.at[0], wr.at[0], partner))

    def norm_step(b, carry):
        rows = pl.ds(pl.multiple_of(b * BLOCK, BLOCK), BLOCK)
        turn = jnp.full((8, SLICE), steps[b], jnp.int32).astype(F32) * (math.pi / 2000.0)
        ca, sa = jnp.cos(turn)[0:1], jnp.sin(turn)[0:1]

        def noisy(j):
            g = xg[j // NY, j % NY, rows, :].astype(F32)
            n = nz[rows, j * SLICE:(j + 1) * SLICE].astype(F32)
            return ca * g + sa * n

        total = jnp.zeros((BLOCK, 1), F32)
        for j in range(16):
            v = noisy(j)
            total = total + jnp.sum(v * v, axis=-1, keepdims=True)
        inv = lax.rsqrt(total * (1.0 / D) + 1e-06)
        for j in range(16):
            xg[j // NY, j % NY, rows, :] = (noisy(j) * inv).astype(BF16)
        return carry

    def norm():
        nz_cp.wait()
        for cp in gx.cp.values():
            cp.wait_send()
        lax.fori_loop(0, ROWS // BLOCK, norm_step, 0)

    def project(h):
        w_own[h].wait()
        acc[...] = jnp.zeros((ROWS, ROWS), F32)

        def proj_step(zz, carry):
            part = jnp.zeros((ROWS, ROWS), F32)
            for cc in range(2):
                s = zz * 2 + cc
                part = part + jnp.dot(
                    xg[s // NY, s % NY], wb[h, zz, cc], preferred_element_type=F32
                )
            acc[...] += part
            return carry

        lax.fori_loop(0, NZ, proj_step, 0)
        q = (rms(acc[:, 0:128]) * gain[0, 0, h]).astype(BF16)
        k = (rms(acc[:, 128:256]) * gain[0, 1, h]).astype(BF16)
        v = acc[:, 256:384].astype(BF16)
        qt[h] = q.reshape(6, BLOCK, HEAD_DIM)
        kv[h][z, c, :, :, 0:128] = k.reshape(6, BLOCK, HEAD_DIM)
        kv[h][z, c, :, :, 128:256] = v.reshape(6, BLOCK, HEAD_DIM)

    sign = (2 * role - 1).astype(F32)
    scale = 1.0 / math.sqrt(HEAD_DIM)

    def attend(h):
        def two_blocks(b2, carry):
            for u in range(2):
                b = b2 * 2 + u
                q = qt[h, b]
                got = []
                for j in range(KMAX):
                    kb = keys[h, b, j]
                    s = kb // 6
                    got.append(kv[h][s // 2, s % 2, kb - s * 6])
                both = jnp.concatenate(got, axis=0)
                s = lax.dot_general(
                    q, both[:, 0:128], (((1,), (1,)), ((), ())), preferred_element_type=F32
                ) * scale
                limit = count[h, b] * BLOCK
                live = lax.broadcasted_iota(jnp.int32, (BLOCK, KMAX * BLOCK), 1) < limit
                s = jnp.where(live, s, -jnp.inf)
                raised = jnp.exp(s - jnp.max(s, axis=-1, keepdims=True))
                w = (raised / jnp.sum(raised, axis=-1, keepdims=True)).astype(BF16)
                mixed = jnp.dot(w, both[:, 128:256], preferred_element_type=F32)
                rows = pl.ds(pl.multiple_of(b * BLOCK, BLOCK), BLOCK)
                at[h, x, y, rows, :] = (mixed * sign).astype(BF16)
            return carry

        lax.fori_loop(0, 3, two_blocks, 0)

    def final(h):
        def final_step(i, carry):
            part = jnp.zeros((ROWS, SLICE), F32)
            for u in range(2):
                j = i * 4 + u * 2
                a = jnp.concatenate([at[h, i, u * 2], at[h, i, u * 2 + 1]], axis=-1)
                part = part + jnp.dot(
                    a, wo[h, pl.ds(j, 2)].reshape(256, SLICE), preferred_element_type=F32
                )
            oacc[...] += part
            return carry

        lax.fori_loop(0, 4, final_step, 0)

    held = []
    oacc[...] = jnp.zeros((ROWS, SLICE), F32)
    wr_[0].own()
    wr_[0].step_a(1)
    wr_[1].own()
    generate()
    gx.start()
    wr_[0].step_b(1)
    cut()
    wr_[0].step_a(2)
    wr_[1].step_a(1)
    gx.one()
    wr_[1].step_b(1)
    gx.two()
    wr_[0].step_b(2)
    wr_[0].step_a(3)
    wr_[2].own()
    wr_[1].step_a(2)
    wr_[1].step_b(2)
    wr_[0].step_b(3)
    gx.three()
    wr_[0].step_a(4)
    wr_[2].step_a(1)
    wr_[0].finish()
    wr_[2].step_b(1)
    gx.four()
    norm()
    wr_[1].step_a(3)
    wr_[1].step_b(3)
    swap_start()
    wr_[2].step_a(2)
    project(0)
    kr_[0].own()
    wr_[2].step_b(2)
    wr_[1].step_a(4)
    wr_[2].step_a(3)
    kr_[0].step_a(1)
    kr_[0].step_b(1)
    wr_[1].finish()
    project(1)
    wr_[2].step_a(4)
    kr_[1].own()
    wr_[2].step_b(3)
    kr_[0].step_a(2)
    kr_[0].step_b(2)
    kr_[1].step_a(1)
    kr_[1].step_b(1)
    wr_[2].finish()
    project(2)
    kr_[2].own()
    kr_[0].step_a(3)
    kr_[0].step_b(3)
    kr_[1].step_a(2)
    kr_[1].step_b(2)
    kr_[2].step_a(1)
    kr_[2].step_b(1)
    kr_[0].step_a(4)
    swap_end()
    kr_[1].step_a(3)
    kr_[0].finish()
    attend(0)
    kr_[1].step_b(3)
    ax[0].start()
    kr_[2].step_a(2)
    kr_[2].step_b(2)
    ax[0].one()
    kr_[1].step_a(4)
    kr_[2].step_a(3)
    ax[0].two()
    kr_[2].step_b(3)
    kr_[2].step_a(4)
    kr_[1].finish()
    attend(1)
    ax[1].start()
    ax[0].three()
    kr_[2].finish()
    attend(2)
    ax[2].start()
    ax[1].one()
    ax[0].four()
    held.pop().wait_recv()
    final(0)
    ax[2].one()
    ax[1].two()
    ax[2].two()
    ax[1].three()
    ax[2].three()
    ax[1].four()
    final(1)
    ax[2].four()
    final(2)
    out[...] = oacc[...].T
    drained = {id(cp) for cp in gx.cp.values()}
    for cp in started:
        if id(cp) not in drained:
            cp.wait_send()


def per_device(
    hidden_rows,
    gen_weight,
    noise,
    timesteps,
    qkv_weight,
    out_weight,
    qk_gain,
    block_keys,
    block_count,
):
    smem = pl.BlockSpec(memory_space=pltpu.SMEM)
    hbm = pl.BlockSpec(memory_space=pl.ANY)
    dma = pltpu.SemaphoreType.DMA
    return pl.pallas_call(
        kernel,
        out_shape=jax.ShapeDtypeStruct((SLICE, ROWS), F32),
        in_specs=[smem] * 4 + [hbm] * 5,
        out_specs=pl.BlockSpec(memory_space=pltpu.VMEM),
        scratch_shapes=[
            pltpu.VMEM((ROWS, D), BF16),
            pltpu.VMEM((SLICE, D), BF16),
            pltpu.VMEM((ROWS, D), BF16),
            pltpu.VMEM((NX, NY, ROWS, SLICE), BF16),
            pltpu.VMEM((HEADS_HERE, NZ, 2, SLICE, ROWS), BF16),
            pltpu.VMEM((HEADS_HERE, 6, BLOCK, HEAD_DIM), BF16),
            *[pltpu.VMEM((NZ, 2, 6, BLOCK, 2 * HEAD_DIM), BF16)] * HEADS_HERE,
            pltpu.VMEM((16, HEADS_HERE, 128, SLICE), BF16),
            pltpu.VMEM((HEADS_HERE, 16, 128, SLICE), BF16),
            pltpu.VMEM((HEADS_HERE, NX, NY, ROWS, HEAD_DIM), BF16),
            pltpu.VMEM((ROWS, ROWS), F32),
            pltpu.VMEM((ROWS, SLICE), F32),
            dma((8,)),
            dma((6, 14)),
            dma((6, 14)),
            dma((6, 9)),
            dma((6, 9)),
            dma((4, 20)),
            dma((4, 20)),
            dma((16,)),
            dma((16,)),
        ],
        compiler_params=pltpu.CompilerParams(
            collective_id=0, has_side_effects=True, vmem_limit_bytes=67043328
        ),
    )(
        timesteps, qk_gain, block_keys, block_count,
        hidden_rows, gen_weight.T, noise, qkv_weight, out_weight,
    ).T


def solution(mesh):
    placed = (
        P("seq", None),
        P(None, ("role", "head")),
        P("seq", None),
        P("seq"),
        P("role", "seq", "head"),
        P("role", "head", None),
        P("role", None, "head"),
        P("head", "seq", None),
        P("head", "seq"),
    )
    return jax.shard_map(
        per_device,
        mesh=mesh,
        in_specs=placed,
        out_specs=P("seq", ("role", "head")),
        check_vma=False,
    )
```

```python
import math

import jax
import jax.numpy as jnp
from jax import lax
from jax.experimental import pallas as pl
from jax.experimental.pallas import tpu as pltpu
from jax.sharding import PartitionSpec as P

HEAD_DIM = 128
BLOCK = 64
KMAX = 8
ROWS = 384
D = 5120
SLICE = 320
NX, NY, NZ = 4, 4, 8
HEADS_HERE = 3
MESH = pl.DeviceIdType.MESH
F32 = jnp.float32
BF16 = jnp.bfloat16


def rms(values):
    return values * lax.rsqrt(jnp.mean(values * values, axis=-1, keepdims=True) + 1e-06)


def kernel(
    steps, gain, keys, count,
    hidden, gen_w, noise, qkv_w, out_w,
    out,
    hid, gw, nz, xg, wb, qt, kv0, kv1, kv2, sl, wo, at, acc, oacc,
    loc_sem, zs, zr, ps, pr, xs, xr, ws, wr,
):
    kv = (kv0, kv1, kv2)
    role = lax.axis_index("role")
    seq = lax.axis_index("seq")
    head = lax.axis_index("head")
    z, c = seq // 2, seq % 2
    x = role * 2 + head // 4
    y = head % 4
    me = x * NY + y

    def at_x(d):
        xx = (x + d + NX) % NX
        return {"role": xx // 2, "head": (xx % 2) * 4 + y}

    def at_y(d):
        return {"head": (head // 4) * 4 + (y + d + NY) % NY}

    def at_z(d, core=c):
        return {"seq": ((z + d + NZ) % NZ) * 2 + core}

    def plane(i):
        j = (me + i) % 16
        return {"role": j // 8, "head": j % 8}

    partner = {"seq": z * 2 + 1 - c}

    barrier = pltpu.get_barrier_semaphore()
    near = [at_z(1), at_z(-1), partner, at_x(1), at_x(-1), at_y(1), at_y(-1)]
    for device in near:
        pl.semaphore_signal(barrier, inc=1, device_id=device, device_id_type=MESH)

    def local(src, dst, i):
        cp = pltpu.make_async_copy(src, dst, loc_sem.at[i])
        cp.start()
        return cp

    w_own = [
        local(qkv_w.at[0, :, pl.ds(h * ROWS, ROWS)], wb.at[h, z, c], h)
        for h in range(HEADS_HERE)
    ]
    hid_cp = local(hidden, hid, 3)
    gw_cp = local(gen_w, gw, 4)
    nz_cp = local(noise, nz, 5)

    pl.semaphore_wait(barrier, len(near))

    started = []

    def send(src, dst, ssem, rsem, device):
        cp = pltpu.make_async_remote_copy(
            src_ref=src, dst_ref=dst, send_sem=ssem, recv_sem=rsem,
            device_id=device, device_id_type=MESH,
        )
        cp.start()
        started.append(cp)
        return cp

    class Ring:
        def __init__(self, g, part, whole, own_part, own_whole):
            self.g, self.part, self.whole = g, part, whole
            self.own_part, self.own_whole = own_part, own_whole
            self.cp = {}

        def push(self, way, half, k):
            shard = (z + NZ - way * (k - 1)) % NZ
            i = (0 if way > 0 else 7) + (k - 1 if half == 0 else (4 if way > 0 else 3) + k - 1)
            ref = self.part(shard, half)
            src = self.own_part(half) if k == 1 else ref
            self.cp[way, half, k] = send(
                src, ref, zs.at[self.g, i], zr.at[self.g, i], at_z(way)
            )
            if k == 4 and self.g == 5:
                n = 7 if way > 0 else 8
                self.cp["p", 4, half] = send(
                    ref, ref, ps.at[self.g, n], pr.at[self.g, n], at_z(way, 1 - c)
                )

        def give(self, d):
            ref = self.whole((z + d + NZ) % NZ)
            n = d + 3
            src = self.own_whole() if d == 0 else ref
            self.cp["p", d] = send(src, ref, ps.at[self.g, n], pr.at[self.g, n], partner)

        def own(self):
            self.push(1, 0, 1)
            self.push(-1, 1, 1)
            self.push(1, 1, 1)
            self.push(-1, 0, 1)
            self.give(0)

        def step_a(self, k):
            for way, half in ((1, 0), (-1, 1)):
                self.cp[way, half, k].wait_recv()
                if k < 4:
                    self.push(way, half, k + 1)
            if k == 4 and self.g < 5:
                self.give(4)

        def step_b(self, k):
            for way, half in ((1, 1), (-1, 0)):
                self.cp[way, half, k].wait_recv()
                if k < 3:
                    self.push(way, half, k + 1)
            self.give(-k)
            self.give(k)

        def finish(self):
            for d in range(-3, 4):
                self.cp["p", d].wait_recv()
            for key in (("p", 4),) if self.g < 5 else (("p", 4, 0), ("p", 4, 1)):
                self.cp[key].wait_recv()

    def w_ring(h):
        return Ring(
            h,
            lambda zz, half: wb.at[h, zz, c, pl.ds(half * 160, 160)],
            lambda zz: wb.at[h, zz, c],
            lambda half: qkv_w.at[0, pl.ds(half * 160, 160), pl.ds(h * ROWS, ROWS)],
            lambda: qkv_w.at[0, :, pl.ds(h * ROWS, ROWS)],
        )

    def kv_ring(h):
        return Ring(
            3 + h,
            lambda zz, half: kv[h].at[zz, c, pl.ds(half * 3, 3)],
            lambda zz: kv[h].at[zz, c],
            lambda half: kv[h].at[z, c, pl.ds(half * 3, 3)],
            lambda: kv[h].at[z, c],
        )

    class Plane:
        def __init__(self, g, buf):
            self.g, self.buf = g, buf
            self.n = 0
            self.cp = {}

        def push(self, name, ref, device):
            self.cp[name] = send(
                ref, ref, xs.at[self.g, self.n], xr.at[self.g, self.n], device
            )
            self.n += 1

        def start(self):
            b = self.buf
            for d in (1, -1):
                self.push(("a1", d), b.at[x, y, pl.ds(0, 192)], at_x(d))
                self.push(("b1", d), b.at[x, y, pl.ds(192, 192)], at_y(d))

        def one(self):
            b = self.buf
            for n, d in enumerate((1, -1)):
                self.cp["a1", d].wait_recv()
                self.push(("a2", d), b.at[(x - d + NX) % NX, y, pl.ds(n * 96, 96)], at_x(d))
                self.cp["b1", d].wait_recv()
                self.push(("b2", d), b.at[x, (y - d + NY) % NY, pl.ds(192 + n * 96, 96)], at_y(d))

        def two(self):
            b = self.buf
            for d in (1, -1):
                self.cp["a2", d].wait_recv()
            for n in (0, 1):
                for d, m in ((1, n), (-1, 1 - n)):
                    self.push(("a3", d, n), b.at[pl.ds(2 * m, 2), y, pl.ds(0, 192)], at_y(d))
            for d in (1, -1):
                self.cp["b2", d].wait_recv()
            for n in (0, 1):
                for d, m in ((1, n), (-1, 1 - n)):
                    self.push(("b3", d, n), b.at[x, pl.ds(2 * m, 2), pl.ds(192, 192)], at_x(d))

        def three(self):
            b = self.buf
            for n, d in enumerate((1, -1)):
                self.cp["a3", d, 0].wait_recv()
                self.push(
                    ("a4", d), b.at[pl.ds(2 * n, 2), (y - d + NY) % NY, pl.ds(0, 192)], at_y(d)
                )
                self.cp["b3", d, 0].wait_recv()
                self.push(
                    ("b4", d), b.at[(x - d + NX) % NX, pl.ds(2 * n, 2), pl.ds(192, 192)], at_x(d)
                )

        def rest(self):
            for d in (1, -1):
                self.cp["a3", d, 1].wait_recv()
                self.cp["b3", d, 1].wait_recv()

        def four(self):
            for d in (1, -1):
                self.cp["a4", d].wait_recv()
                self.cp["b4", d].wait_recv()

    wr_ = [w_ring(h) for h in range(HEADS_HERE)]
    kr_ = [kv_ring(h) for h in range(HEADS_HERE)]
    gx = Plane(0, xg)
    ax = [Plane(1 + h, at.at[h]) for h in range(HEADS_HERE)]

    def gen_step(i, carry):
        k0 = pl.multiple_of(i * 1024, 1024)
        acc[:, :SLICE] += lax.dot_general(
            hid[:, pl.ds(k0, 1024)], gw[:, pl.ds(k0, 1024)],
            (((1,), (1,)), ((), ())), preferred_element_type=F32,
        )
        return carry

    def generate():
        hid_cp.wait()
        gw_cp.wait()
        acc[:, :SLICE] = jnp.zeros((ROWS, SLICE), F32)
        lax.fori_loop(0, D // 1024, gen_step, 0)
        xg[x, y] = acc[:, :SLICE].astype(BF16)
        held.append(local(out_w.at[0], hid, 6))

    def cut():
        held.pop().wait()
        for j in range(16):
            sl[j] = hid[:, j * SLICE:(j + 1) * SLICE].reshape(HEADS_HERE, 128, SLICE)

    half = pl.ds(c * 64, 64)
    wo_own = pltpu.make_async_copy(sl.at[me, :, half], wo.at[:, me, half], loc_sem.at[7])

    def wo_copy(i):
        j = (me + i) % 16
        return pltpu.make_async_remote_copy(
            src_ref=sl.at[j, :, half], dst_ref=wo.at[:, me, half],
            send_sem=ws.at[i], recv_sem=wr.at[i],
            device_id=plane(i), device_id_type=MESH,
        )

    def wo_start(i, carry):
        wo_copy(i).start()
        return carry

    def wo_wait(i, carry):
        wo_copy(i).wait()
        return carry

    def swap_start():
        wo_own.start()
        lax.fori_loop(1, 16, wo_start, 0)

    def swap_end():
        wo_own.wait()
        lax.fori_loop(1, 16, wo_wait, 0)
        held.append(send(wo.at[:, :, half], wo.at[:, :, half], ws.at[0], wr.at[0], partner))

    def norm_step(b, carry):
        rows = pl.ds(pl.multiple_of(b * BLOCK, BLOCK), BLOCK)
        turn = jnp.full((8, SLICE), steps[b], jnp.int32).astype(F32) * (math.pi / 2000.0)
        ca, sa = jnp.cos(turn)[0:1], jnp.sin(turn)[0:1]

        def noisy(j):
            g = xg[j // NY, j % NY, rows, :].astype(F32)
            n = nz[rows, j * SLICE:(j + 1) * SLICE].astype(F32)
            return ca * g + sa * n

        total = jnp.zeros((BLOCK, 1), F32)
        for j in range(16):
            v = noisy(j)
            total = total + jnp.sum(v * v, axis=-1, keepdims=True)
        inv = lax.rsqrt(total * (1.0 / D) + 1e-06)
        for j in range(16):
            xg[j // NY, j % NY, rows, :] = (noisy(j) * inv).astype(BF16)
        return carry

    def norm():
        nz_cp.wait()
        for cp in gx.cp.values():
            cp.wait_send()
        lax.fori_loop(0, ROWS // BLOCK, norm_step, 0)

    def project(h):
        w_own[h].wait()
        acc[...] = jnp.zeros((ROWS, ROWS), F32)

        def proj_step(zz, carry):
            part = jnp.zeros((ROWS, ROWS), F32)
            for cc in range(2):
                s = zz * 2 + cc
                part = part + jnp.dot(
                    xg[s // NY, s % NY], wb[h, zz, cc], preferred_element_type=F32
                )
            acc[...] += part
            return carry

        lax.fori_loop(0, NZ, proj_step, 0)
        q = (rms(acc[:, 0:128]) * gain[0, 0, h]).astype(BF16)
        k = (rms(acc[:, 128:256]) * gain[0, 1, h]).astype(BF16)
        v = acc[:, 256:384].astype(BF16)
        qt[h] = q.reshape(6, BLOCK, HEAD_DIM)
        kv[h][z, c, :, :, 0:128] = k.reshape(6, BLOCK, HEAD_DIM)
        kv[h][z, c, :, :, 128:256] = v.reshape(6, BLOCK, HEAD_DIM)

    sign = (2 * role - 1).astype(F32)
    scale = 1.0 / math.sqrt(HEAD_DIM)

    def attend(h):
        def two_blocks(b2, carry):
            for u in range(2):
                b = b2 * 2 + u
                q = qt[h, b]
                got = []
                for j in range(KMAX):
                    kb = keys[h, b, j]
                    s = kb // 6
                    got.append(kv[h][s // 2, s % 2, kb - s * 6])
                both = jnp.concatenate(got, axis=0)
                s = lax.dot_general(
                    q, both[:, 0:128], (((1,), (1,)), ((), ())), preferred_element_type=F32
                ) * scale
                limit = count[h, b] * BLOCK
                live = lax.broadcasted_iota(jnp.int32, (BLOCK, KMAX * BLOCK), 1) < limit
                s = jnp.where(live, s, -jnp.inf)
                raised = jnp.exp(s - jnp.max(s, axis=-1, keepdims=True))
                w = (raised / jnp.sum(raised, axis=-1, keepdims=True)).astype(BF16)
                mixed = jnp.dot(w, both[:, 128:256], preferred_element_type=F32)
                rows = pl.ds(pl.multiple_of(b * BLOCK, BLOCK), BLOCK)
                at[h, x, y, rows, :] = (mixed * sign).astype(BF16)
            return carry

        lax.fori_loop(0, 3, two_blocks, 0)

    def final(h):
        def final_step(i, carry):
            part = jnp.zeros((ROWS, SLICE), F32)
            for u in range(2):
                j = i * 4 + u * 2
                a = jnp.concatenate([at[h, i, u * 2], at[h, i, u * 2 + 1]], axis=-1)
                part = part + jnp.dot(
                    a, wo[h, pl.ds(j, 2)].reshape(256, SLICE), preferred_element_type=F32
                )
            oacc[...] += part
            return carry

        lax.fori_loop(0, 4, final_step, 0)

    held = []
    def final_at(h, off):
        top, low = pl.ds(0, 192), pl.ds(192, 192)
        for p in (0, 2):
            yy = (y + off) % NY
            a = jnp.concatenate([at[h, p, yy, top, :], at[h, p + 1, yy, top, :]], axis=-1)
            w = jnp.concatenate([wo[h, p * NY + yy], wo[h, (p + 1) * NY + yy]], axis=0)
            oacc[top, :] += jnp.dot(a, w, preferred_element_type=F32)
            xx = (x + off) % NX
            a = jnp.concatenate([at[h, xx, p, low, :], at[h, xx, p + 1, low, :]], axis=-1)
            w = wo[h, pl.ds(xx * NY + p, 2)].reshape(256, SLICE)
            oacc[low, :] += jnp.dot(a, w, preferred_element_type=F32)

    oacc[...] = jnp.zeros((ROWS, SLICE), F32)
    wr_[0].own()
    wr_[0].step_a(1)
    wr_[1].own()
    generate()
    gx.start()
    wr_[0].step_b(1)
    cut()
    wr_[0].step_a(2)
    wr_[1].step_a(1)
    gx.one()
    wr_[1].step_b(1)
    gx.two()
    wr_[0].step_b(2)
    wr_[0].step_a(3)
    wr_[2].own()
    wr_[1].step_a(2)
    wr_[1].step_b(2)
    wr_[0].step_b(3)
    gx.three()
    wr_[0].step_a(4)
    wr_[2].step_a(1)
    wr_[0].finish()
    wr_[2].step_b(1)
    gx.rest()
    gx.four()
    norm()
    wr_[1].step_a(3)
    wr_[1].step_b(3)
    swap_start()
    wr_[2].step_a(2)
    project(0)
    kr_[0].own()
    wr_[2].step_b(2)
    wr_[1].step_a(4)
    wr_[2].step_a(3)
    kr_[0].step_a(1)
    kr_[0].step_b(1)
    wr_[1].finish()
    project(1)
    wr_[2].step_a(4)
    kr_[1].own()
    wr_[2].step_b(3)
    kr_[0].step_a(2)
    kr_[0].step_b(2)
    kr_[1].step_a(1)
    kr_[1].step_b(1)
    wr_[2].finish()
    project(2)
    kr_[2].own()
    kr_[0].step_a(3)
    kr_[0].step_b(3)
    kr_[1].step_a(2)
    kr_[1].step_b(2)
    kr_[2].step_a(1)
    kr_[2].step_b(1)
    kr_[0].step_a(4)
    swap_end()
    kr_[1].step_a(3)
    kr_[0].finish()
    attend(0)
    kr_[1].step_b(3)
    ax[0].start()
    kr_[2].step_a(2)
    kr_[2].step_b(2)
    ax[0].one()
    kr_[1].step_a(4)
    kr_[2].step_a(3)
    ax[0].two()
    kr_[2].step_b(3)
    kr_[2].step_a(4)
    kr_[1].finish()
    attend(1)
    ax[1].start()
    ax[0].three()
    kr_[2].finish()
    attend(2)
    ax[2].start()
    ax[1].one()
    ax[0].rest()
    ax[0].four()
    held.pop().wait_recv()
    final(0)
    ax[2].one()
    ax[1].two()
    ax[2].two()
    ax[1].three()
    ax[2].three()
    final_at(2, 0)
    ax[2].rest()
    final_at(2, 1)
    final_at(2, 3)
    ax[1].rest()
    ax[1].four()
    final(1)
    ax[2].four()
    final_at(2, 2)
    out[...] = oacc[...].T
    drained = {id(cp) for cp in gx.cp.values()}
    for cp in started:
        if id(cp) not in drained:
            cp.wait_send()


def per_device(
    hidden_rows,
    gen_weight,
    noise,
    timesteps,
    qkv_weight,
    out_weight,
    qk_gain,
    block_keys,
    block_count,
):
    smem = pl.BlockSpec(memory_space=pltpu.SMEM)
    hbm = pl.BlockSpec(memory_space=pl.ANY)
    dma = pltpu.SemaphoreType.DMA
    return pl.pallas_call(
        kernel,
        out_shape=jax.ShapeDtypeStruct((SLICE, ROWS), F32),
        in_specs=[smem] * 4 + [hbm] * 5,
        out_specs=pl.BlockSpec(memory_space=pltpu.VMEM),
        scratch_shapes=[
            pltpu.VMEM((ROWS, D), BF16),
            pltpu.VMEM((SLICE, D), BF16),
            pltpu.VMEM((ROWS, D), BF16),
            pltpu.VMEM((NX, NY, ROWS, SLICE), BF16),
            pltpu.VMEM((HEADS_HERE, NZ, 2, SLICE, ROWS), BF16),
            pltpu.VMEM((HEADS_HERE, 6, BLOCK, HEAD_DIM), BF16),
            *[pltpu.VMEM((NZ, 2, 6, BLOCK, 2 * HEAD_DIM), BF16)] * HEADS_HERE,
            pltpu.VMEM((16, HEADS_HERE, 128, SLICE), BF16),
            pltpu.VMEM((HEADS_HERE, 16, 128, SLICE), BF16),
            pltpu.VMEM((HEADS_HERE, NX, NY, ROWS, HEAD_DIM), BF16),
            pltpu.VMEM((ROWS, ROWS), F32),
            pltpu.VMEM((ROWS, SLICE), F32),
            dma((8,)),
            dma((6, 14)),
            dma((6, 14)),
            dma((6, 9)),
            dma((6, 9)),
            dma((4, 20)),
            dma((4, 20)),
            dma((16,)),
            dma((16,)),
        ],
        compiler_params=pltpu.CompilerParams(
            collective_id=0, has_side_effects=True, vmem_limit_bytes=67043328
        ),
    )(
        timesteps, qk_gain, block_keys, block_count,
        hidden_rows, gen_weight.T, noise, qkv_weight, out_weight,
    ).T


def solution(mesh):
    placed = (
        P("seq", None),
        P(None, ("role", "head")),
        P("seq", None),
        P("seq"),
        P("role", "seq", "head"),
        P("role", "head", None),
        P("role", None, "head"),
        P("head", "seq", None),
        P("head", "seq"),
    )
    return jax.shard_map(
        per_device,
        mesh=mesh,
        in_specs=placed,
        out_specs=P("seq", ("role", "head")),
        check_vma=False,
    )
```

```python
import math

import jax
import jax.numpy as jnp
from jax import lax
from jax.experimental import pallas as pl
from jax.experimental.pallas import tpu as pltpu
from jax.sharding import PartitionSpec as P

HEAD_DIM = 128
BLOCK = 64
KMAX = 8
ROWS = 384
D = 5120
SLICE = 320
NX, NY, NZ = 4, 4, 8
HEADS_HERE = 3
MESH = pl.DeviceIdType.MESH
F32 = jnp.float32
BF16 = jnp.bfloat16


def rms(values):
    return values * lax.rsqrt(jnp.mean(values * values, axis=-1, keepdims=True) + 1e-06)


def kernel(
    steps, gain, keys, count,
    hidden, gen_w, noise, qkv_w, out_w,
    out,
    hid, gw, nz, xg, wb, qt, kv0, kv1, kv2, sl, wo, at, acc, oacc,
    loc_sem, zs, zr, ps, pr, xs, xr, ws, wr,
):
    kv = (kv0, kv1, kv2)
    role = lax.axis_index("role")
    seq = lax.axis_index("seq")
    head = lax.axis_index("head")
    z, c = seq // 2, seq % 2
    x = role * 2 + head // 4
    y = head % 4
    me = x * NY + y

    def at_x(d):
        xx = (x + d + NX) % NX
        return {"role": xx // 2, "head": (xx % 2) * 4 + y}

    def at_y(d):
        return {"head": (head // 4) * 4 + (y + d + NY) % NY}

    def at_z(d, core=c):
        return {"seq": ((z + d + NZ) % NZ) * 2 + core}

    def plane(i):
        j = (me + i) % 16
        return {"role": j // 8, "head": j % 8}

    partner = {"seq": z * 2 + 1 - c}

    barrier = pltpu.get_barrier_semaphore()
    near = [at_z(1), at_z(-1), partner, at_x(1), at_x(-1), at_y(1), at_y(-1)]
    for device in near:
        pl.semaphore_signal(barrier, inc=1, device_id=device, device_id_type=MESH)

    def local(src, dst, i):
        cp = pltpu.make_async_copy(src, dst, loc_sem.at[i])
        cp.start()
        return cp

    w_own = [
        local(qkv_w.at[0, :, pl.ds(h * ROWS, ROWS)], wb.at[h, z, c], h)
        for h in range(HEADS_HERE)
    ]
    hid_cp = local(hidden, hid, 3)
    gw_cp = local(gen_w, gw, 4)
    nz_cp = local(noise, nz, 5)

    pl.semaphore_wait(barrier, len(near))

    started = []

    def send(src, dst, ssem, rsem, device):
        cp = pltpu.make_async_remote_copy(
            src_ref=src, dst_ref=dst, send_sem=ssem, recv_sem=rsem,
            device_id=device, device_id_type=MESH,
        )
        cp.start()
        started.append(cp)
        return cp

    class Ring:
        def __init__(self, g, part, whole, own_part, own_whole):
            self.g, self.part, self.whole = g, part, whole
            self.own_part, self.own_whole = own_part, own_whole
            self.cp = {}

        def push(self, way, half, k):
            shard = (z + NZ - way * (k - 1)) % NZ
            i = (0 if way > 0 else 7) + (k - 1 if half == 0 else (4 if way > 0 else 3) + k - 1)
            ref = self.part(shard, half)
            src = self.own_part(half) if k == 1 else ref
            self.cp[way, half, k] = send(
                src, ref, zs.at[self.g, i], zr.at[self.g, i], at_z(way)
            )
            if k == 4 and self.g == 5:
                n = 7 if way > 0 else 8
                self.cp["p", 4, half] = send(
                    ref, ref, ps.at[self.g, n], pr.at[self.g, n], at_z(way, 1 - c)
                )

        def give(self, d):
            ref = self.whole((z + d + NZ) % NZ)
            n = d + 3
            src = self.own_whole() if d == 0 else ref
            self.cp["p", d] = send(src, ref, ps.at[self.g, n], pr.at[self.g, n], partner)

        def own(self):
            self.push(1, 0, 1)
            self.push(-1, 1, 1)
            self.push(1, 1, 1)
            self.push(-1, 0, 1)
            self.give(0)

        def step_a(self, k):
            for way, half in ((1, 0), (-1, 1)):
                self.cp[way, half, k].wait_recv()
                if k < 4:
                    self.push(way, half, k + 1)
            if k == 4 and self.g < 5:
                self.give(4)

        def step_b(self, k):
            for way, half in ((1, 1), (-1, 0)):
                self.cp[way, half, k].wait_recv()
                if k < 3:
                    self.push(way, half, k + 1)
            self.give(-k)
            self.give(k)

        def finish(self):
            for d in range(-3, 4):
                self.cp["p", d].wait_recv()
            for key in (("p", 4),) if self.g < 5 else (("p", 4, 0), ("p", 4, 1)):
                self.cp[key].wait_recv()

    def w_ring(h):
        return Ring(
            h,
            lambda zz, half: wb.at[h, zz, c, pl.ds(half * 160, 160)],
            lambda zz: wb.at[h, zz, c],
            lambda half: qkv_w.at[0, pl.ds(half * 160, 160), pl.ds(h * ROWS, ROWS)],
            lambda: qkv_w.at[0, :, pl.ds(h * ROWS, ROWS)],
        )

    def kv_ring(h):
        return Ring(
            3 + h,
            lambda zz, half: kv[h].at[zz, c, pl.ds(half * 3, 3)],
            lambda zz: kv[h].at[zz, c],
            lambda half: kv[h].at[z, c, pl.ds(half * 3, 3)],
            lambda: kv[h].at[z, c],
        )

    class Plane:
        def __init__(self, g, buf):
            self.g, self.buf = g, buf
            self.n = 0
            self.cp = {}

        def push(self, name, ref, device):
            self.cp[name] = send(
                ref, ref, xs.at[self.g, self.n], xr.at[self.g, self.n], device
            )
            self.n += 1

        def start(self):
            b = self.buf
            for d in (1, -1):
                self.push(("a1", d), b.at[x, y, pl.ds(0, 192)], at_x(d))
                self.push(("b1", d), b.at[x, y, pl.ds(192, 192)], at_y(d))

        def one(self):
            b = self.buf
            for n, d in enumerate((1, -1)):
                self.cp["a1", d].wait_recv()
                self.push(("a2", d), b.at[(x - d + NX) % NX, y, pl.ds(n * 96, 96)], at_x(d))
                self.cp["b1", d].wait_recv()
                self.push(("b2", d), b.at[x, (y - d + NY) % NY, pl.ds(192 + n * 96, 96)], at_y(d))

        def two(self):
            b = self.buf
            for d in (1, -1):
                self.cp["a2", d].wait_recv()
            for n in (0, 1):
                for d, m in ((1, n), (-1, 1 - n)):
                    self.push(("a3", d, n), b.at[pl.ds(2 * m, 2), y, pl.ds(0, 192)], at_y(d))
            for d in (1, -1):
                self.cp["b2", d].wait_recv()
            for n in (0, 1):
                for d, m in ((1, n), (-1, 1 - n)):
                    self.push(("b3", d, n), b.at[x, pl.ds(2 * m, 2), pl.ds(192, 192)], at_x(d))

        def three(self):
            b = self.buf
            for n, d in enumerate((1, -1)):
                self.cp["a3", d, 0].wait_recv()
                self.push(
                    ("a4", d), b.at[pl.ds(2 * n, 2), (y - d + NY) % NY, pl.ds(0, 192)], at_y(d)
                )
                self.cp["b3", d, 0].wait_recv()
                self.push(
                    ("b4", d), b.at[(x - d + NX) % NX, pl.ds(2 * n, 2), pl.ds(192, 192)], at_x(d)
                )

        def rest(self):
            for d in (1, -1):
                self.cp["a3", d, 1].wait_recv()
                self.cp["b3", d, 1].wait_recv()

        def four(self):
            for d in (1, -1):
                self.cp["a4", d].wait_recv()
                self.cp["b4", d].wait_recv()

    wr_ = [w_ring(h) for h in range(HEADS_HERE)]
    kr_ = [kv_ring(h) for h in range(HEADS_HERE)]
    gx = Plane(0, xg)
    ax = [Plane(1 + h, at.at[h]) for h in range(HEADS_HERE)]

    def gen_step(i, carry):
        k0 = pl.multiple_of(i * 1024, 1024)
        acc[:, :SLICE] += lax.dot_general(
            hid[:, pl.ds(k0, 1024)], gw[:, pl.ds(k0, 1024)],
            (((1,), (1,)), ((), ())), preferred_element_type=F32,
        )
        return carry

    def generate():
        hid_cp.wait()
        gw_cp.wait()
        acc[:, :SLICE] = jnp.zeros((ROWS, SLICE), F32)
        lax.fori_loop(0, D // 1024, gen_step, 0)
        xg[x, y] = acc[:, :SLICE].astype(BF16)
        held.append(local(out_w.at[0], hid, 6))

    def cut():
        held.pop().wait()
        for j in range(16):
            sl[j] = hid[:, j * SLICE:(j + 1) * SLICE].reshape(HEADS_HERE, 128, SLICE)

    half = pl.ds(c * 64, 64)
    wo_own = pltpu.make_async_copy(sl.at[me, :, half], wo.at[:, me, half], loc_sem.at[7])

    def wo_copy(i):
        j = (me + i) % 16
        return pltpu.make_async_remote_copy(
            src_ref=sl.at[j, :, half], dst_ref=wo.at[:, me, half],
            send_sem=ws.at[i], recv_sem=wr.at[i],
            device_id=plane(i), device_id_type=MESH,
        )

    def wo_start(i, carry):
        wo_copy(i).start()
        return carry

    def wo_wait(i, carry):
        wo_copy(i).wait()
        return carry

    def swap_start():
        wo_own.start()
        lax.fori_loop(1, 16, wo_start, 0)

    def swap_end():
        wo_own.wait()
        lax.fori_loop(1, 16, wo_wait, 0)
        held.append(send(wo.at[:, :, half], wo.at[:, :, half], ws.at[0], wr.at[0], partner))

    def norm_step(b, carry):
        rows = pl.ds(pl.multiple_of(b * BLOCK, BLOCK), BLOCK)
        turn = jnp.full((8, SLICE), steps[b], jnp.int32).astype(F32) * (math.pi / 2000.0)
        ca, sa = jnp.cos(turn)[0:1], jnp.sin(turn)[0:1]

        def noisy(j):
            g = xg[j // NY, j % NY, rows, :].astype(F32)
            n = nz[rows, j * SLICE:(j + 1) * SLICE].astype(F32)
            return ca * g + sa * n

        total = jnp.zeros((BLOCK, 1), F32)
        for j in range(16):
            v = noisy(j)
            total = total + jnp.sum(v * v, axis=-1, keepdims=True)
        inv = lax.rsqrt(total * (1.0 / D) + 1e-06)
        for j in range(16):
            xg[j // NY, j % NY, rows, :] = (noisy(j) * inv).astype(BF16)
        return carry

    def norm():
        nz_cp.wait()
        for cp in gx.cp.values():
            cp.wait_send()
        lax.fori_loop(0, ROWS // BLOCK, norm_step, 0)

    def project(h):
        w_own[h].wait()
        acc[...] = jnp.zeros((ROWS, ROWS), F32)

        def proj_step(zz, carry):
            part = jnp.zeros((ROWS, ROWS), F32)
            for cc in range(2):
                s = zz * 2 + cc
                part = part + jnp.dot(
                    xg[s // NY, s % NY], wb[h, zz, cc], preferred_element_type=F32
                )
            acc[...] += part
            return carry

        lax.fori_loop(0, NZ, proj_step, 0)
        q = (rms(acc[:, 0:128]) * gain[0, 0, h]).astype(BF16)
        k = (rms(acc[:, 128:256]) * gain[0, 1, h]).astype(BF16)
        v = acc[:, 256:384].astype(BF16)
        qt[h] = q.reshape(6, BLOCK, HEAD_DIM)
        kv[h][z, c, :, :, 0:128] = k.reshape(6, BLOCK, HEAD_DIM)
        kv[h][z, c, :, :, 128:256] = v.reshape(6, BLOCK, HEAD_DIM)

    sign = (2 * role - 1).astype(F32)
    scale = 1.0 / math.sqrt(HEAD_DIM)

    def attend(h):
        def two_blocks(b2, carry):
            for u in range(2):
                b = b2 * 2 + u
                q = qt[h, b]
                got = []
                for j in range(KMAX):
                    kb = keys[h, b, j]
                    s = kb // 6
                    got.append(kv[h][s // 2, s % 2, kb - s * 6])
                both = jnp.concatenate(got, axis=0)
                s = lax.dot_general(
                    q, both[:, 0:128], (((1,), (1,)), ((), ())), preferred_element_type=F32
                ) * scale
                limit = count[h, b] * BLOCK
                live = lax.broadcasted_iota(jnp.int32, (BLOCK, KMAX * BLOCK), 1) < limit
                s = jnp.where(live, s, -jnp.inf)
                raised = jnp.exp(s - jnp.max(s, axis=-1, keepdims=True))
                w = (raised / jnp.sum(raised, axis=-1, keepdims=True)).astype(BF16)
                mixed = jnp.dot(w, both[:, 128:256], preferred_element_type=F32)
                rows = pl.ds(pl.multiple_of(b * BLOCK, BLOCK), BLOCK)
                at[h, x, y, rows, :] = (mixed * sign).astype(BF16)
            return carry

        lax.fori_loop(0, 3, two_blocks, 0)

    def final(h):
        def final_step(i, carry):
            part = jnp.zeros((ROWS, SLICE), F32)
            for u in range(2):
                j = i * 4 + u * 2
                a = jnp.concatenate([at[h, i, u * 2], at[h, i, u * 2 + 1]], axis=-1)
                part = part + jnp.dot(
                    a, wo[h, pl.ds(j, 2)].reshape(256, SLICE), preferred_element_type=F32
                )
            oacc[...] += part
            return carry

        lax.fori_loop(0, 4, final_step, 0)

    held = []
    def final_at(h, off):
        top, low = pl.ds(0, 192), pl.ds(192, 192)
        for p in (0, 2):
            yy = (y + off) % NY
            a = jnp.concatenate([at[h, p, yy, top, :], at[h, p + 1, yy, top, :]], axis=-1)
            w = jnp.concatenate([wo[h, p * NY + yy], wo[h, (p + 1) * NY + yy]], axis=0)
            oacc[top, :] += jnp.dot(a, w, preferred_element_type=F32)
            xx = (x + off) % NX
            a = jnp.concatenate([at[h, xx, p, low, :], at[h, xx, p + 1, low, :]], axis=-1)
            w = wo[h, pl.ds(xx * NY + p, 2)].reshape(256, SLICE)
            oacc[low, :] += jnp.dot(a, w, preferred_element_type=F32)

    oacc[...] = jnp.zeros((ROWS, SLICE), F32)
    wr_[0].own()
    wr_[0].step_a(1)
    wr_[1].own()
    generate()
    gx.start()
    wr_[0].step_b(1)
    cut()
    wr_[0].step_a(2)
    wr_[1].step_a(1)
    gx.one()
    wr_[1].step_b(1)
    gx.two()
    wr_[0].step_b(2)
    wr_[0].step_a(3)
    wr_[2].own()
    wr_[1].step_a(2)
    wr_[1].step_b(2)
    wr_[0].step_b(3)
    gx.three()
    wr_[0].step_a(4)
    wr_[2].step_a(1)
    wr_[0].finish()
    wr_[2].step_b(1)
    gx.rest()
    gx.four()
    norm()
    wr_[1].step_a(3)
    wr_[1].step_b(3)
    swap_start()
    wr_[2].step_a(2)
    project(0)
    kr_[0].own()
    wr_[2].step_b(2)
    wr_[1].step_a(4)
    wr_[2].step_a(3)
    kr_[0].step_a(1)
    kr_[0].step_b(1)
    wr_[1].finish()
    project(1)
    wr_[2].step_a(4)
    kr_[1].own()
    wr_[2].step_b(3)
    kr_[0].step_a(2)
    kr_[0].step_b(2)
    kr_[1].step_a(1)
    kr_[1].step_b(1)
    wr_[2].finish()
    project(2)
    kr_[0].step_a(3)
    kr_[0].step_b(3)
    kr_[2].own()
    kr_[1].step_a(2)
    kr_[1].step_b(2)
    kr_[2].step_a(1)
    kr_[2].step_b(1)
    kr_[0].step_a(4)
    swap_end()
    kr_[1].step_a(3)
    kr_[0].finish()
    attend(0)
    kr_[1].step_b(3)
    ax[0].start()
    kr_[2].step_a(2)
    kr_[2].step_b(2)
    ax[0].one()
    kr_[1].step_a(4)
    kr_[2].step_a(3)
    ax[0].two()
    kr_[2].step_b(3)
    kr_[2].step_a(4)
    kr_[1].finish()
    attend(1)
    ax[1].start()
    ax[0].three()
    kr_[2].finish()
    attend(2)
    ax[2].start()
    ax[1].one()
    ax[0].rest()
    ax[0].four()
    held.pop().wait_recv()
    final(0)
    ax[2].one()
    ax[1].two()
    ax[2].two()
    ax[1].three()
    ax[2].three()
    final_at(2, 0)
    ax[2].rest()
    final_at(2, 1)
    final_at(2, 3)
    ax[1].rest()
    ax[1].four()
    final(1)
    ax[2].four()
    final_at(2, 2)
    out[...] = oacc[...].T
    drained = {id(cp) for cp in gx.cp.values()}
    for cp in started:
        if id(cp) not in drained:
            cp.wait_send()


def per_device(
    hidden_rows,
    gen_weight,
    noise,
    timesteps,
    qkv_weight,
    out_weight,
    qk_gain,
    block_keys,
    block_count,
):
    smem = pl.BlockSpec(memory_space=pltpu.SMEM)
    hbm = pl.BlockSpec(memory_space=pl.ANY)
    dma = pltpu.SemaphoreType.DMA
    return pl.pallas_call(
        kernel,
        out_shape=jax.ShapeDtypeStruct((SLICE, ROWS), F32),
        in_specs=[smem] * 4 + [hbm] * 5,
        out_specs=pl.BlockSpec(memory_space=pltpu.VMEM),
        scratch_shapes=[
            pltpu.VMEM((ROWS, D), BF16),
            pltpu.VMEM((SLICE, D), BF16),
            pltpu.VMEM((ROWS, D), BF16),
            pltpu.VMEM((NX, NY, ROWS, SLICE), BF16),
            pltpu.VMEM((HEADS_HERE, NZ, 2, SLICE, ROWS), BF16),
            pltpu.VMEM((HEADS_HERE, 6, BLOCK, HEAD_DIM), BF16),
            *[pltpu.VMEM((NZ, 2, 6, BLOCK, 2 * HEAD_DIM), BF16)] * HEADS_HERE,
            pltpu.VMEM((16, HEADS_HERE, 128, SLICE), BF16),
            pltpu.VMEM((HEADS_HERE, 16, 128, SLICE), BF16),
            pltpu.VMEM((HEADS_HERE, NX, NY, ROWS, HEAD_DIM), BF16),
            pltpu.VMEM((ROWS, ROWS), F32),
            pltpu.VMEM((ROWS, SLICE), F32),
            dma((8,)),
            dma((6, 14)),
            dma((6, 14)),
            dma((6, 9)),
            dma((6, 9)),
            dma((4, 20)),
            dma((4, 20)),
            dma((16,)),
            dma((16,)),
        ],
        compiler_params=pltpu.CompilerParams(
            collective_id=0, has_side_effects=True, vmem_limit_bytes=67043328
        ),
    )(
        timesteps, qk_gain, block_keys, block_count,
        hidden_rows, gen_weight.T, noise, qkv_weight, out_weight,
    ).T


def solution(mesh):
    placed = (
        P("seq", None),
        P(None, ("role", "head")),
        P("seq", None),
        P("seq"),
        P("role", "seq", "head"),
        P("role", "head", None),
        P("role", None, "head"),
        P("head", "seq", None),
        P("head", "seq"),
    )
    return jax.shard_map(
        per_device,
        mesh=mesh,
        in_specs=placed,
        out_specs=P("seq", ("role", "head")),
        check_vma=False,
    )
```
